32 devices in a mesh: section: 2 (over y), node: 4 (over z), lane: 4 (over x, core).
Axes of the slice: x: 2, y: 2, z: 4, core: 2. Of those that a mesh axis runs over, the one named last changes fastest.
Arguments:
- forward_input: bfloat16 [2, 1024, 2048], P('section', ('node', 'lane')), may hold values from -6 to 6
- forward_routes: int32 [2, 1024, 8], P('section', ('node', 'lane')), may hold values from 0 to 15, all different within a row; in each aligned block of 64 rows (0 to 63, 64 to 127, ..., all dimensions but the last counted through in order) at most 36 rows name the same one
- forward_gates: float32 [2, 1024, 8], P('section', ('node', 'lane')), may hold values from 0.05 to 0.4
- backward_input: bfloat16 [2, 1024, 2048], P('section', ('node', 'lane')), may hold values from -6 to 6
- backward_cotangent: bfloat16 [2, 1024, 2048], P('section', ('node', 'lane')), may hold values from -6 to 6
- backward_routes: int32 [2, 1024, 8], P('section', ('node', 'lane')), may hold values from 0 to 15, all different within a row; in each aligned block of 64 rows (0 to 63, 64 to 127, ..., all dimensions but the last counted through in order) at most 36 rows name the same one
- backward_gates: float32 [2, 1024, 8], P('section', ('node', 'lane')), may hold values from 0.05 to 0.4
- w_gate: bfloat16 [2, 16, 2048, 768], P('section', ('node', 'lane')), may hold values from -0.125 to 0.125
- w_up: bfloat16 [2, 16, 2048, 768], P('section', ('node', 'lane')), may hold values from -0.125 to 0.125
- w_down: bfloat16 [2, 16, 768, 2048], P('section', ('node', 'lane')), may hold values from -0.21875 to 0.21875
Outputs:
- next_input: bfloat16 [2, 1024, 2048], P('section', ('node', 'lane'))
- previous_gradient: bfloat16 [2, 1024, 2048], P('section', ('node', 'lane'))
The draws below stay inside these ranges and needn't reach their ends.
Inputs may be any that keep to these rules, and one draw needn't show every extreme that they name: `forward_routes`: each row names 8 different experts. Within the 64 rows of one device (aligned blocks), no expert is named by more than 36 rows, a bound that some block reaches. `backward_routes`: each row names 8 different experts. Within the 64 rows of one device (aligned blocks), no expert is named by more than 36 rows, a bound that some block reaches.
All inputs are finite; a program needn't handle non-finite values.
Results may differ from the reference program's by a relative error of at most 0.0064.
Values may be sent and summed in bfloat16 or wider, within the bound.
A program may use at most 128 MiB of HBM per device.

```python
import math
import jax
import jax.numpy as jnp
import numpy as np
from jax import lax

D = 2048
FF = 768
TOPK = 8
TOK_DEV = 64
EXPERTS = 16
TOKENS = 1024
CAP = 36
N_SECTION = 2
N_NODE = 4
N_LANE = 4


def shard_levels(rng, shape, cuts, smallest, top_value):
    gain = 1.0
    for position, blocks in cuts:
        steps = jax.random.uniform(jax.random.fold_in(jax.random.fold_in(rng, 6), position), (blocks,), jnp.float32, smallest / len(cuts), top_value / len(cuts))
        gain = gain * jnp.repeat(jnp.exp(steps), shape[position] // blocks).reshape((-1,) + (1,) * (len(shape) - 1 - position))
    return gain


def shared_out(key, own, number, rows, count, top, most, skew):
    ranking = jax.random.permutation(key, count)
    heavy_load, ordinary = portions_of(count, rows * top, most, skew, True), portions_of(count, rows * top, most, skew, False)
    places = jnp.arange(count)

    def named(sizes, turn):
        used = int((sizes > 0).sum())
        fixed = max(1, used // 4)
        passed = fixed + (places - fixed + turn * (used - fixed)) % max(1, count - fixed)
        return jnp.zeros((count,), jnp.int32).at[ranking[jnp.where(places < fixed, places, passed)]].set(jnp.asarray(sizes, jnp.int32))

    sizes = jnp.where(number % 4 == 0, named(heavy_load, number // 4), named(ordinary, number - number // 4 - 1))
    mixed = jax.random.permutation(jax.random.fold_in(own, 3), count)
    donor, sink = mixed[0:count // 2 * 2:2], mixed[1:count // 2 * 2:2]
    room = jnp.minimum(sizes[donor] - 1, most - sizes[sink]) // 2
    room = jnp.where((donor == ranking[0]) | (sink == ranking[0]) | (sizes[sink] == 0), 0, jnp.maximum(room, 0))
    passed = jax.random.randint(jax.random.fold_in(own, 4), (count // 2,), 0, 1 << 20) % (room + 1)
    sizes = sizes.at[donor].add(-passed).at[sink].add(passed)
    items = jnp.searchsorted(jnp.cumsum(sizes), jnp.arange(rows * top), side="right").astype(jnp.int32)
    grid = items.reshape(top, rows).T
    grid = grid[jax.random.permutation(jax.random.fold_in(own, 1), rows)]
    turn = jax.random.randint(jax.random.fold_in(own, 2), (rows, 1), 0, top)
    return jnp.take_along_axis(grid, (jnp.arange(top)[None, :] + turn) % top, axis=1)


def portions_of(number_of, total, bound, skew, full):
    weights = [(1 << 20) // math.isqrt(rank ** skew) + 1 for rank in range(1, number_of + 1)]
    largest = bound if full else min(bound, max(-(-total // number_of), total * weights[0] // sum(weights)))
    least = 1 if total - largest >= number_of - 1 else 0
    given, rest = [largest] + [least] * (number_of - 1), total - largest - least * (number_of - 1)
    while rest > 0:
        free = [i for i in range(1, number_of) if given[i] < largest] or [i for i in range(1, number_of) if given[i] < bound]
        mass, remaining = sum([weights[i] for i in free]), rest
        for i in free:
            extra = min(bound - given[i], max(1, remaining * weights[i] // mass), rest)
            given[i] = given[i] + extra
            rest = rest - extra
    return np.array(given)


def noise(rng, extent, spread, most, split=(), held_as=jnp.bfloat16):
    level = shard_levels(rng, extent, split, -0.22, 0.18) if split else 1.0
    entries = jax.random.normal(rng, extent, jnp.float32) * spread * level
    return jnp.minimum(jnp.maximum(entries, -most), most).astype(held_as)


def setup_inputs(seed: int = 0) -> dict:
    splits = jax.random.split(jax.random.key(seed), 11)
    forward_input = noise(splits[0], (N_SECTION, TOKENS, D), 1.0, 6.0, ((0, 2), (1, 16)))
    forward_routes_keys = jax.random.split(jax.random.fold_in(splits[1], 1), N_SECTION * TOKENS // TOK_DEV)
    forward_routes_turns = jax.random.permutation(jax.random.fold_in(splits[1], 3), N_SECTION * TOKENS // TOK_DEV)
    forward_routes = jax.vmap(lambda own, number: shared_out(jax.random.fold_in(splits[1], 2), own, number, TOK_DEV, EXPERTS, TOPK, CAP, 1))(forward_routes_keys, forward_routes_turns).reshape((N_SECTION, TOKENS, TOPK))
    forward_gates = jnp.clip(jnp.exp(math.log(0.4) - 2.0794415 * jax.random.uniform(splits[2], (N_SECTION, TOKENS, TOPK), jnp.float32) ** shard_levels(splits[2], (N_SECTION, TOKENS, TOPK), ((0, 2), (1, 16)), -0.2, 0.2)), 0.05, 0.4)
    backward_input = noise(splits[3], (N_SECTION, TOKENS, D), 1.0, 6.0, ((0, 2), (1, 16)))
    backward_cotangent = noise(splits[4], (N_SECTION, TOKENS, D), 1.0, 6.0, ((0, 2), (1, 16)))
    backward_routes_keys = jax.random.split(jax.random.fold_in(splits[5], 1), N_SECTION * TOKENS // TOK_DEV)
    backward_routes_turns = jax.random.permutation(jax.random.fold_in(splits[5], 3), N_SECTION * TOKENS // TOK_DEV)
    backward_routes = jax.vmap(lambda own, number: shared_out(jax.random.fold_in(splits[5], 2), own, number, TOK_DEV, EXPERTS, TOPK, CAP, 1))(backward_routes_keys, backward_routes_turns).reshape((N_SECTION, TOKENS, TOPK))
    backward_gates = jnp.clip(jnp.exp(math.log(0.4) - 2.0794415 * jax.random.uniform(splits[6], (N_SECTION, TOKENS, TOPK), jnp.float32) ** shard_levels(splits[6], (N_SECTION, TOKENS, TOPK), ((0, 2), (1, 16)), -0.2, 0.2)), 0.05, 0.4)
    w_gate = noise(splits[7], (N_SECTION, EXPERTS, D, FF), D ** -0.5, 0.125, ((0, 2), (1, 16)))
    w_up = noise(splits[8], (N_SECTION, EXPERTS, D, FF), D ** -0.5, 0.125, ((0, 2), (1, 16)))
    w_down = noise(splits[9], (N_SECTION, EXPERTS, FF, D), FF ** -0.5, 0.21875, ((0, 2), (1, 16)))
    return {"forward_input": forward_input, "forward_routes": forward_routes, "forward_gates": forward_gates, "backward_input": backward_input, "backward_cotangent": backward_cotangent, "backward_routes": backward_routes, "backward_gates": backward_gates, "w_gate": w_gate, "w_up": w_up, "w_down": w_down}


def expert_forward(rows, w_g, w_u, w_d):
    pre_gate = jnp.dot(rows, w_g, preferred_element_type=jnp.float32)
    pre_up = jnp.dot(rows, w_u, preferred_element_type=jnp.float32)
    hidden = (jax.nn.silu(pre_gate) * pre_up).astype(jnp.bfloat16)
    return jnp.dot(hidden, w_d, preferred_element_type=jnp.float32).astype(jnp.bfloat16)


def expert_backward(rows, grads, w_g, w_u, w_d):
    pre_gate = jnp.dot(rows, w_g, preferred_element_type=jnp.float32)
    pre_up = jnp.dot(rows, w_u, preferred_element_type=jnp.float32)
    grad_hidden = lax.dot_general(grads, w_d, (((1,), (1,)), ((), ())), preferred_element_type=jnp.float32)
    sigma = jax.nn.sigmoid(pre_gate)
    grad_gate = (grad_hidden * pre_up * sigma * (1.0 + pre_gate * (1.0 - sigma))).astype(jnp.bfloat16)
    grad_up = (grad_hidden * pre_gate * sigma).astype(jnp.bfloat16)
    total = lax.dot_general(grad_gate, w_g, (((1,), (1,)), ((), ())), preferred_element_type=jnp.float32)
    total = total + lax.dot_general(grad_up, w_u, (((1,), (1,)), ((), ())), preferred_element_type=jnp.float32)
    return total.astype(jnp.bfloat16)


def slot_index(routes):
    sources = N_NODE * N_LANE
    blocks = routes.reshape(sources, TOK_DEV * TOPK).astype(jnp.int32)
    onehot = (blocks[:, :, None] == jnp.arange(EXPERTS, dtype=jnp.int32)[None, None, :]).astype(jnp.int32)
    before = jnp.cumsum(onehot, axis=1) - onehot
    slot = jnp.sum(before * onehot, axis=2).astype(jnp.int32)
    anchor = jnp.arange(sources, dtype=jnp.int32)[:, None]
    return (blocks * (sources * CAP) + anchor * CAP + slot).reshape(-1).astype(jnp.int32)


def place(rows, index):
    buffer = jnp.zeros((EXPERTS * N_NODE * N_LANE * CAP, D), jnp.bfloat16)
    return buffer.at[index].set(rows).reshape(EXPERTS, N_NODE * N_LANE * CAP, D)


def forward_layer(tokens, routes, gates, w_g, w_u, w_d):
    index = slot_index(routes)
    buffer = place(jnp.repeat(tokens, TOPK, axis=0), index)
    outputs = lax.map(lambda item: expert_forward(*item), (buffer, w_g, w_u, w_d))
    picked = outputs.reshape(-1, D)[index].reshape(TOKENS, TOPK, D).astype(jnp.float32)
    return jnp.sum(picked * gates[:, :, None].astype(jnp.float32), axis=1).astype(jnp.bfloat16)


def backward_layer(tokens, cotangent, routes, gates, w_g, w_u, w_d):
    index = slot_index(routes)
    rows = place(jnp.repeat(tokens, TOPK, axis=0), index)
    scaled = (gates.reshape(-1)[:, None].astype(jnp.float32) * jnp.repeat(cotangent, TOPK, axis=0).astype(jnp.float32)).astype(jnp.bfloat16)
    grads = place(scaled, index)
    pieces = lax.map(lambda item: expert_backward(*item), (rows, grads, w_g, w_u, w_d))
    picked = pieces.reshape(-1, D)[index].reshape(TOKENS, TOPK, D).astype(jnp.float32)
    return jnp.sum(picked, axis=1).astype(jnp.bfloat16)


def reference(forward_input, forward_routes, forward_gates, backward_input, backward_cotangent, backward_routes, backward_gates, w_gate, w_up, w_down):
    outs_forward = []
    outs_backward = []
    for section in range(N_SECTION):
        outs_forward.append(forward_layer(forward_input[section], forward_routes[section], forward_gates[section], w_gate[section], w_up[section], w_down[section]))
        outs_backward.append(backward_layer(backward_input[section], backward_cotangent[section], backward_routes[section], backward_gates[section], w_gate[section], w_up[section], w_down[section]))
    layer_out = jnp.stack(outs_forward)
    input_grad = jnp.stack(outs_backward)
    return jnp.roll(layer_out, 1, axis=0), jnp.roll(input_grad, -1, axis=0)
```

```python
import functools
import math

import jax
import jax.numpy as jnp
from jax import lax
from jax.experimental import pallas as pl
from jax.experimental.pallas import tpu as pltpu
from jax.sharding import PartitionSpec as P

GROUP = ("node", "lane")
CORES = 2
MESH = pl.DeviceIdType.MESH


def position():
    node, lane = lax.axis_index("node"), lax.axis_index("lane")
    return node, lane // CORES, lane % CORES


def greet(peers):
    barrier = pltpu.get_barrier_semaphore()
    for cond, device in peers:
        @pl.when(cond)
        def _():
            pl.semaphore_signal(barrier, inc=1, device_id=device, device_id_type=MESH)
    pl.semaphore_wait(barrier, sum(jnp.where(cond, 1, 0) for cond, _ in peers))


def gather_kernel(n_node, n_x, count, *refs):
    ins, outs = refs[:count], refs[count : 2 * count]
    local_sem, recv, z_sem, x_sem, core_sem = refs[2 * count :]
    node, x, core = position()
    lane = x * CORES + core
    z_up, z_down = {"node": node + 1}, {"node": node - 1}
    x_up, x_down = {"lane": lane + CORES}, {"lane": lane - CORES}
    partner = {"lane": lane + 1 - 2 * core}
    has_up, has_down = node < n_node - 1, node > 0
    has_right, has_left = x < n_x - 1, x > 0
    greet(
        [
            (has_up, z_up),
            (has_down, z_down),
            (has_right, x_up),
            (has_left, x_down),
            (core < CORES, partner),
        ]
    )
    sends = []

    def send(cond, a, src, z, at_x, sem, device):
        where = outs[a].at[z, at_x * CORES + core]

        def copy():
            return pltpu.make_async_remote_copy(
                src_ref=where if src is None else src,
                dst_ref=where,
                send_sem=sem,
                recv_sem=recv.at[a, z, at_x * CORES + core],
                device_id=device,
                device_id_type=MESH,
            )

        @pl.when(cond)
        def _():
            copy().start()

        sends.append((cond, copy))

    def arrived(a, z, at_lane):
        where = outs[a].at[z, at_lane]
        pltpu.make_async_remote_copy(
            src_ref=where,
            dst_ref=where,
            send_sem=core_sem.at[a, 0, 0],
            recv_sem=recv.at[a, z, at_lane],
            device_id=partner,
            device_id_type=MESH,
        ).wait_recv()

    def along_x(cond, a, src, z):
        send(cond & has_right, a, src, z, x, x_sem.at[a, 0, z, x], x_up)
        send(cond & has_left, a, src, z, x, x_sem.at[a, 1, z, x], x_down)
        send(cond, a, src, z, x, core_sem.at[a, z, x], partner)

    always = core < CORES
    keeps = []
    for a in range(count):
        send(has_up, a, ins[a], node, x, z_sem.at[a, 0, node], z_up)
        send(has_down, a, ins[a], node, x, z_sem.at[a, 1, node], z_down)
        along_x(always, a, ins[a], node)
    for a in range(count):
        keep = pltpu.make_async_copy(ins[a], outs[a].at[node, lane], local_sem.at[a])
        keep.start()
        keeps.append(keep)
    for step in range(1, n_node):
        for a in range(count):
            below, above = node - step, node + step
            from_below, from_above = below >= 0, above < n_node

            @pl.when(from_below)
            def _():
                arrived(a, below, lane)

            send(from_below & has_up, a, None, below, x, z_sem.at[a, 0, below], z_up)
            along_x(from_below, a, None, below)

            @pl.when(from_above)
            def _():
                arrived(a, above, lane)

            send(from_above & has_down, a, None, above, x, z_sem.at[a, 1, above], z_down)
            along_x(from_above, a, None, above)
    for step in range(1, n_x):
        for a in range(count):
            for k in range(n_node):
                z = (node + k) % n_node
                for at_x, cond, go_on, way, device in (
                    (x - step, x - step >= 0, has_right, 0, x_up),
                    (x + step, x + step < n_x, has_left, 1, x_down),
                ):
                    @pl.when(cond)
                    def _():
                        arrived(a, z, at_x * CORES + core)

                    if n_x > 2:
                        send(cond & go_on, a, None, z, at_x, x_sem.at[a, way, z, at_x], device)
                    send(cond, a, None, z, at_x, core_sem.at[a, z, at_x], partner)
    for a in range(count):
        for k in range(n_node):
            for at_x in range(n_x):
                arrived(a, k, at_x * CORES + 1 - core)
    for cond, copy in sends:
        @pl.when(cond)
        def _():
            copy().wait_send()
    for keep in keeps:
        keep.wait()


def gather(*arrays):
    n_node, n_lane = lax.axis_size("node"), lax.axis_size("lane")
    n_x, count = n_lane // CORES, len(arrays)
    return pl.pallas_call(
        functools.partial(gather_kernel, n_node, n_x, count),
        out_shape=[jax.ShapeDtypeStruct((n_node, n_lane) + a.shape, a.dtype) for a in arrays],
        in_specs=[pl.BlockSpec(memory_space=pltpu.VMEM)] * count,
        out_specs=[pl.BlockSpec(memory_space=pl.ANY)] * count,
        scratch_shapes=[
            pltpu.SemaphoreType.DMA((count,)),
            pltpu.SemaphoreType.DMA((count, n_node, n_lane)),
            pltpu.SemaphoreType.DMA((count, 2, n_node)),
            pltpu.SemaphoreType.DMA((count, 2, n_node, n_x)),
            pltpu.SemaphoreType.DMA((count, n_node, n_x)),
        ],
        compiler_params=pltpu.CompilerParams(collective_id=0, has_side_effects=True),
    )(*arrays)


def scatter_kernel(n_section, n_node, n_x, count, *refs):
    parts, outs = refs[:count], refs[count : 2 * count]
    (own, core_in, x_in, z_in, final, local_sem, core_send, core_recv, x_send, x_recv, z_send,
     z_recv, y_send, y_recv) = refs[2 * count :]
    node, x, core = position()
    section = lax.axis_index("section")
    lane = x * CORES + core
    partner = {"lane": lane + 1 - 2 * core}
    z_up, z_down = {"node": node + 1}, {"node": node - 1}
    x_up, x_down = {"lane": lane + CORES}, {"lane": lane - CORES}
    after = {"section": (section + 1) % n_section}
    before = {"section": (section + n_section - 1) % n_section}
    has_up, has_down = node < n_node - 1, node > 0
    has_right, has_left = x < n_x - 1, x > 0
    always = core < CORES
    greet(
        [
            (has_up, z_up),
            (has_down, z_down),
            (has_right, x_up),
            (has_left, x_down),
            (always, partner),
            (always, after),
            (always, before),
        ]
    )

    def remote(src, dst, send_sem, recv_sem, device):
        return pltpu.make_async_remote_copy(
            src_ref=src,
            dst_ref=dst,
            send_sem=send_sem,
            recv_sem=recv_sem,
            device_id=device,
            device_id_type=MESH,
        )

    def add(target, *others):
        total = target[...].astype(jnp.float32)
        for other in others:
            total = total + other[...].astype(jnp.float32)
        target[...] = total.astype(target.dtype)

    sends = []

    def start(cond, make):
        @pl.when(cond)
        def _():
            make().start()

        sends.append((cond, make))

    owners = []
    for t in range(n_node - 1):
        owners.append((node + n_node - 1 - t, t >= node))
        owners.append((t + node - (n_node - 1), t + node >= n_node - 1))
    x_steps = [
        (t, x + n_x - 1 - t, t >= x, t + x - (n_x - 1), t + x >= n_x - 1) for t in range(n_x - 1)
    ]
    every = owners + [(node, always)]

    loads = []
    for a in range(count):
        load = pltpu.make_async_copy(parts[a].at[:, :, core], own.at[a], local_sem.at[a])
        load.start()
        loads.append(load)

    def core_copy(a, z, at_x):
        return remote(
            parts[a].at[z, at_x, 1 - core],
            core_in.at[a, z, at_x],
            core_send.at[a, z, at_x],
            core_recv.at[a, z, at_x],
            partner,
        )

    for a in range(count):
        for z, cond in every:
            for _, q_up, c_up, q_down, c_down in x_steps:
                start(cond & c_up, functools.partial(core_copy, a, z, q_up))
                start(cond & c_down, functools.partial(core_copy, a, z, q_down))
        for z, cond in every:
            start(cond, functools.partial(core_copy, a, z, x))

    def x_copy(a, z, q, slot, device):
        return remote(
            own.at[a, z, q], x_in.at[a, z, slot], x_send.at[a, z, q], x_recv.at[a, z, slot], device
        )

    def z_copy(a, z, slot, device):
        return remote(
            own.at[a, z, x], z_in.at[a, slot], z_send.at[a, z], z_recv.at[a, slot], device
        )

    for a in range(count):
        loads[a].wait()
        for z, cond in every:
            for t, q_up, c_up, q_down, c_down in x_steps:
                for q, c, more, slot, device in (
                    (q_up, c_up, has_left, q_up, x_up),
                    (q_down, c_down, has_right, None, x_down),
                ):
                    @pl.when(cond & c)
                    def _():
                        core_copy(a, z, q).wait_recv()
                        add(own.at[a, z, q], core_in.at[a, z, q])

                    if t > 0:
                        @pl.when(cond & c & more)
                        def _():
                            x_copy(a, z, q, q, partner).wait_recv()
                            add(own.at[a, z, q], x_in.at[a, z, q])

                    if slot is not None:
                        start(cond & c, functools.partial(x_copy, a, z, q, slot, device))
                    else:
                        near = q == x - 1
                        start(
                            cond & c & near, functools.partial(x_copy, a, z, q, n_x, device)
                        )
                        if n_x > 2:
                            start(
                                cond & c & (q < x - 1),
                                functools.partial(x_copy, a, z, q, q, device),
                            )

    def collect(a, z):
        core_copy(a, z, x).wait_recv()
        add(own.at[a, z, x], core_in.at[a, z, x])
        for c, slot in ((has_left, x), (has_right, n_x)):
            @pl.when(c)
            def _():
                x_copy(a, z, 0, slot, partner).wait_recv()
                add(own.at[a, z, x], x_in.at[a, z, slot])

    for a in range(count):
        for k, (z, cond) in enumerate(owners):
            going_up = k % 2 == 0

            @pl.when(cond)
            def _():
                collect(a, z)

            if k >= 2:
                @pl.when(cond & (has_down if going_up else has_up))
                def _():
                    z_copy(a, z, z, partner).wait_recv()
                    add(own.at[a, z, x], z_in.at[a, z])

            if going_up:
                start(cond, functools.partial(z_copy, a, z, z, z_up))
            else:
                start(cond & (z == node - 1), functools.partial(z_copy, a, z, n_node, z_down))
                if n_node > 2:
                    start(cond & (z < node - 1), functools.partial(z_copy, a, z, z, z_down))
        collect(a, node)

    def y_copy(a):
        return remote(
            final.at[a], outs[a], y_send.at[a], y_recv.at[a], after if a == 0 else before
        )

    for a in range(count):
        for c, slot in ((has_down, node), (has_up, n_node)):
            @pl.when(c)
            def _():
                z_copy(a, node, slot, partner).wait_recv()
                add(own.at[a, node, x], z_in.at[a, slot])
        final[a] = own[a, node, x]
        y_copy(a).start()
    for a in range(count):
        y_copy(a).wait()
    for cond, make in sends:
        @pl.when(cond)
        def _():
            make().wait_send()


def scatter(*parts):
    n_section, n_node = lax.axis_size("section"), lax.axis_size("node")
    n_x, count = lax.axis_size("lane") // CORES, len(parts)
    rows, width = parts[0].shape
    tok = rows // (n_node * n_x * CORES)
    dtype = parts[0].dtype
    block = (tok, width)
    dma = pltpu.SemaphoreType.DMA
    return pl.pallas_call(
        functools.partial(scatter_kernel, n_section, n_node, n_x, count),
        out_shape=[jax.ShapeDtypeStruct(block, dtype)] * count,
        in_specs=[pl.BlockSpec(memory_space=pl.ANY)] * count,
        out_specs=[pl.BlockSpec(memory_space=pltpu.VMEM)] * count,
        scratch_shapes=[
            pltpu.VMEM((count, n_node, n_x) + block, dtype),
            pltpu.VMEM((count, n_node, n_x) + block, dtype),
            pltpu.VMEM((count, n_node, n_x + 1) + block, dtype),
            pltpu.VMEM((count, n_node + 1) + block, dtype),
            pltpu.VMEM((count,) + block, dtype),
            dma((count,)),
            dma((count, n_node, n_x)),
            dma((count, n_node, n_x)),
            dma((count, n_node, n_x)),
            dma((count, n_node, n_x + 1)),
            dma((count, n_node)),
            dma((count, n_node + 1)),
            dma((count,)),
            dma((count,)),
        ],
        compiler_params=pltpu.CompilerParams(
            collective_id=1, has_side_effects=True, vmem_limit_bytes=67043328
        ),
    )(*(part.reshape((n_node, n_x, CORES) + block) for part in parts))


def coefficients(routes, gates, experts):
    hit = routes[:, :, None] == jnp.arange(experts, dtype=jnp.int32)[None, None, :]
    return jnp.sum(jnp.where(hit, gates[:, :, None], 0.0), axis=1)


def contract_last(a, b):
    return lax.dot_general(a, b, (((1,), (1,)), ((), ())), preferred_element_type=jnp.float32)


VMEM_BYTES = 64 * 2**20
ROW_TILE = 16
LANES = 128


def distance_order(n):
    return [sorted(range(n), key=lambda other: (abs(other - z), (z >= n // 2) != (other > z))) for z in range(n)]


def fused_kernel(shape, *refs):
    n_section, n_node, experts, tok, cross, plan = shape
    (f_in, f_routes, f_gates, b_in, cot_in, b_routes, b_gates, wg_in, wu_in, wd_in) = refs[:10]
    outs = refs[10:12]
    (rows, coefs, routes, gates, w_g, w_u, w_d, hid_a, hid_b) = refs[12:21]
    n_items = 3
    parts, core_in, x_in, z_in, last = (refs[21 + n_items * k : 21 + n_items * (k + 1)] for k in range(5))
    (ls, zs, zr, xs, xr, cs, cr, es, er, rs, rr, hs, hr, ys, yr) = refs[21 + 5 * n_items :]
    half = tok // 2
    node, x, core = position()
    section = lax.axis_index("section")
    lane = x * CORES + core
    me = node * (2 * CORES) + lane
    z_up, z_down = {"node": node + 1}, {"node": node - 1}
    beside = {"lane": (1 - x) * CORES + core}
    partner = {"lane": lane + 1 - 2 * core}
    after = {"section": (section + 1) % n_section}
    before = {"section": (section + n_section - 1) % n_section}
    has_up, has_down = node < n_node - 1, node > 0
    always = core < CORES
    order = distance_order(n_node)

    def near(k):
        found = order[0][k]
        for z in range(1, n_node):
            found = jnp.where(node == z, order[z][k], found)
        return found

    loads = []

    def load(src, dst):
        loads.append(pltpu.make_async_copy(src, dst, ls.at[len(loads)]))
        loads[-1].start()
        return loads[-1]

    small = [load(f_routes, routes.at[0]), load(b_routes, routes.at[1]),
             load(f_gates, gates.at[0]), load(b_gates, gates.at[1])]
    own = [[load(f_in, rows.at[0, node, x, core])]]
    for h in range(2):
        own.append(
            [
                load(b_in.at[pl.ds(h * half, half)], rows.at[1 + h, node, x, core, pl.ds(0, half)]),
                load(cot_in.at[pl.ds(h * half, half)], rows.at[1 + h, node, x, core, pl.ds(half, half)]),
            ]
        )
    weights = [load(wg_in, w_g), load(wu_in, w_u), load(wd_in, w_d)]

    for copy in small:
        copy.wait()
    groups = LANES // (2 * experts)
    held = tok // groups
    at = lax.broadcasted_iota(jnp.int32, (held, LANES), 1)
    packed = jnp.zeros((held, LANES), jnp.float32)
    for which in range(2):
        for g in range(groups):
            some = slice(g * held, (g + 1) * held)
            for k in range(routes.shape[2]):
                chosen = at == routes[which, some, k : k + 1] + (g * 2 + which) * experts
                packed = packed + jnp.where(chosen, gates[which, some, k : k + 1], 0.0)
    coefs[node, x, core] = packed

    greet(
        [
            (has_up, z_up),
            (has_down, z_down),
            (always, beside),
            (always, partner),
            (always, after),
            (always, before),
        ]
    )

    pending = []

    def remote(src, dst, send_sem, recv_sem, device):
        return pltpu.make_async_remote_copy(
            src_ref=src, dst_ref=dst, send_sem=send_sem, recv_sem=recv_sem,
            device_id=device, device_id_type=MESH,
        )

    def start(cond, make):
        if cond is None:
            make().start()
        else:
            @pl.when(cond)
            def _():
                make().start()
        pending.append((cond, make))

    def drain(keep=0):
        while len(pending) > keep:
            cond, make = pending.pop(0)
            if cond is None:
                make().wait_send()
            else:
                @pl.when(cond)
                def _():
                    make().wait_send()

    n_coef = n_items
    T1 = pl.ds(0, tok - cross)
    T2 = pl.ds(tok - cross, cross)

    def block(i, z, at_x, at_core=None):
        at_core = core if at_core is None else at_core
        return coefs.at[z, at_x, at_core] if i == n_coef else rows.at[i, z, at_x, at_core]

    def z_piece(i, z, p):
        return rows.at[i, z, 1 - x, core, T2] if p else block(i, z, x)

    def x_piece(i, z, at_x, whole):
        return block(i, z, at_x) if whole or i == n_coef else rows.at[i, z, at_x, core, T1]

    def z_copy(i, z, p, slot, device):
        where = z_piece(i, z, p)
        return remote(where, where, zs.at[i, slot, p], zr.at[i, z, p], device)

    def x_copy(i, z, at_x, whole):
        where = x_piece(i, z, at_x, whole)
        return remote(where, where, xs.at[i, z], xr.at[i, z], beside)

    def c_copy(i, z, at_x, at_core, q):
        where = block(i, z, at_x, at_core)
        return remote(where, where, cs.at[i, z, q], cr.at[i, z, q], partner)

    both = functools.partial

    def along_z(i, z, p):
        start(has_up, both(z_copy, i, z, p, z, z_up))
        start(has_down, both(z_copy, i, z, p, n_node, z_down))

    def members(i):
        return (n_coef, i) if i == 0 else (i,)

    def sides(j):
        return (
            (node - j, node - j >= 0, has_up, z_up),
            (node + j, node + j < n_node, has_down, z_down),
        )

    def arrive_z(i, j):
        if j == 0:
            for copy in own[i]:
                copy.wait()
            for m in members(i):
                along_z(m, node, 0)
                start(None, both(x_copy, m, node, x, True))
                start(None, both(c_copy, m, node, x, core, 0))
            return
        for p in range(2):
            for z, there, go, device in sides(j):
                for m in members(i):
                    if p and (m == n_coef or not cross):
                        continue

                    @pl.when(there)
                    def _():
                        z_copy(m, z, p, z, device).wait_recv()

                    start(there & go, both(z_copy, m, z, p, z, device))
                    if p == 0:
                        start(there, both(x_copy, m, z, x, False))
                        start(there, both(c_copy, m, z, x, core, 0))

    def arrive_x(i, j):
        if j == 0:
            for m in members(i):
                x_copy(m, node, 1 - x, True).wait_recv()
                if m != n_coef and cross:
                    along_z(m, node, 1)
                start(None, both(c_copy, m, node, 1 - x, core, 1))
            return
        for z, there, _, _ in sides(j):
            for m in members(i):
                @pl.when(there)
                def _():
                    x_copy(m, z, 1 - x, False).wait_recv()

                start(there, both(c_copy, m, z, 1 - x, core, 1))

    def exchange(i, z, at_x):
        return remote(
            parts[i].at[z, at_x, 1 - core], core_in[i].at[z, at_x],
            es.at[i, z, at_x], er.at[i, z, at_x], partner,
        )

    def coef_of(z, which, first, count):
        where = lax.broadcasted_iota(jnp.int32, (held, LANES), 1)
        columns = []
        for at_x in range(2):
            for at_core in range(CORES):
                values = coefs[z, at_x, at_core]
                for g in range(first // held, (first + count) // held):
                    wanted = where == g * (2 * experts) + which * experts + me
                    columns.append(jnp.sum(jnp.where(wanted, values, 0.0), axis=1, keepdims=True))
        return jnp.concatenate(columns, axis=0)

    ff, width = w_d.shape
    wide = 512 if width % 512 == 0 else width

    def forward(z):
        count = 2 * CORES * tok
        coef = coef_of(z, 0, 0, tok)

        def down(j):
            js = pl.ds(pl.multiple_of(j * wide, wide), wide)
            out = jnp.dot(hid_a[...], w_d[:, js], preferred_element_type=jnp.float32) * coef
            parts[0][z, :, :, :, js] = out.astype(jnp.bfloat16).reshape(2, CORES, tok, wide)

        def hidden(j):
            js = pl.ds(pl.multiple_of(j * 256, 256), 256)
            v = rows[0, z].reshape(count, width)
            a = jnp.dot(v, w_g[:, js], preferred_element_type=jnp.float32)
            b = jnp.dot(v, w_u[:, js], preferred_element_type=jnp.float32)
            hid_a[:, js] = (a / (1.0 + jnp.exp(-a)) * b).astype(jnp.bfloat16)

        pl.loop(0, ff // 256)(hidden)
        pl.loop(0, width // wide)(down)

    def backward(i, z):
        count = 2 * CORES * half
        coef = coef_of(z, 1, (i - 1) * half, half)

        def hidden(j):
            js = pl.ds(pl.multiple_of(j * 256, 256), 256)
            v = rows[i, z, :, :, 0:half].reshape(count, width)
            g = rows[i, z, :, :, half:].reshape(count, width)
            a = jnp.dot(v, w_g[:, js], preferred_element_type=jnp.float32)
            b = jnp.dot(v, w_u[:, js], preferred_element_type=jnp.float32)
            h = contract_last(g, w_d[js, :]) * coef
            q = 1.0 / (1.0 + jnp.exp(-a))
            hid_a[0:count, js] = (h * b * q * (1.0 + a * (1.0 - q))).astype(jnp.bfloat16)
            hid_b[0:count, js] = (h * a * q).astype(jnp.bfloat16)

        def down(j):
            js = pl.ds(pl.multiple_of(j * wide, wide), wide)
            total = contract_last(hid_a[0:count], w_g[js, :]) + contract_last(hid_b[0:count], w_u[js, :])
            parts[i][z, :, :, :, js] = total.astype(jnp.bfloat16).reshape(2, CORES, half, wide)

        pl.loop(0, ff // 256)(hidden)
        pl.loop(0, width // wide)(down)

    def compute(i, k):
        if (i, k) == (0, 0):
            for copy in weights:
                copy.wait()
        z = near(k)
        for m in members(i):
            c_copy(m, z, x, 1 - core, 0).wait_recv()
            c_copy(m, z, 1 - x, 1 - core, 1).wait_recv()
        forward(z) if i == 0 else backward(i, z)
        for at_x in (1 - x, x):
            start(None, both(exchange, i, z, at_x))

    def total_of(*terms):
        total = terms[0].astype(jnp.float32)
        for term in terms[1:]:
            total = total + term.astype(jnp.float32)
        return total.astype(jnp.bfloat16)

    def r_copy(i, z):
        return remote(parts[i].at[z, 1 - x, core], x_in[i].at[z], rs.at[i, z], rr.at[i, z], beside)

    def cross_x(i, k):
        z = near(k)
        exchange(i, z, 1 - x).wait_recv()
        parts[i][z, 1 - x, core] = total_of(parts[i][z, 1 - x, core], core_in[i][z, 1 - x])
        start(None, both(r_copy, i, z))

    def h_copy(i, z, way):
        return remote(
            parts[i].at[z, x, core], z_in[i].at[way, z], hs.at[i, z], hr.at[i, way, z],
            (z_up, z_down)[way],
        )

    def y_copy(i):
        a = 0 if i == 0 else 1
        dst = outs[0] if i == 0 else outs[1].at[pl.ds((i - 1) * half, half)]
        return remote(last[i], dst, ys.at[i], yr.at[i], after if a == 0 else before)

    def chain(i, s):
        if s == n_node - 1:
            exchange(i, node, x).wait_recv()
            r_copy(i, node).wait_recv()
            for ways, there in (((0,), node == n_node - 1), ((1,), node == 0), ((0, 1), has_down & has_up)):
                @pl.when(there)
                def _():
                    for way in ways:
                        h_copy(i, node, way).wait_recv()
                    arrived = [z_in[i][way, node] for way in ways]
                    terms = [parts[i][node, x, core], core_in[i][node, x], x_in[i][node]]
                    last[i][...] = total_of(*terms, *arrived)

            y_copy(i).start()
            return
        for way, z, there, more in (
            (0, n_node - 1 + node - s, s >= node, has_down),
            (1, s + node - (n_node - 1), s + node >= n_node - 1, has_up),
        ):
            @pl.when(there)
            def _():
                exchange(i, z, x).wait_recv()
                r_copy(i, z).wait_recv()

            def mine():
                return [parts[i][z, x, core], core_in[i][z, x], x_in[i][z]]

            @pl.when(there & more)
            def _():
                h_copy(i, z, way).wait_recv()
                parts[i][z, x, core] = total_of(*mine(), z_in[i][way, z])

            @pl.when(there & (node == (n_node - 1) * way))
            def _():
                parts[i][z, x, core] = total_of(*mine())

            start(there, both(h_copy, i, z, way))

    for step in plan:
        kind, i, k = step
        if kind == "D":
            drain(k)
        else:
            {"A": arrive_z, "X": arrive_x, "C": compute, "R": cross_x, "H": chain}[kind](i, k)
    for i in range(n_items):
        y_copy(i).wait()
    drain()


def schedule(n):
    far = n - 1
    a = lambda i, j: ("A", i, j)
    xx = lambda i, j: ("X", i, j)
    c = lambda i, j: ("C", i, j)
    r = lambda i, j: ("R", i, j)
    h = lambda i, j: ("H", i, j)
    d = lambda keep: ("D", 0, keep)
    plan = [a(0, 0), xx(0, 0)]
    for j in range(1, far):
        plan += [a(0, j), c(0, j - 1), xx(0, j), r(0, j - 1)]
    plan += [a(0, far), a(1, 0), c(0, far - 1), xx(0, far), xx(1, 0), r(0, far - 1)]
    for i in (1, 2):
        chain = [h(i - 1, s) for s in range(n)]
        older = [h(i - 2, n - 1)] if i == 2 else []
        plan += [a(i, 1), c(i - 1, far), xx(i, 1), r(i - 1, far)] + older + [c(i, 0)]
        for j in range(2, far):
            plan += [a(i, j), c(i, j - 1), xx(i, j), r(i, j - 2), d(40)]
            plan += chain[:1]
            chain = chain[1:]
        plan += [a(i, far)] + ([a(i + 1, 0)] if i == 1 else [])
        plan += [c(i, far - 1), xx(i, far)] + ([xx(i + 1, 0)] if i == 1 else [])
        plan += [r(i, far - 2), r(i, far - 1), d(40)]
        plan += chain[: len(chain) - 1] if i == 1 else chain[:1]
        chain = chain[len(chain) - 1 :] if i == 1 else chain[1:]
    plan += [c(2, far)] + chain[:-1] + [r(2, far)] + chain[-1:] + [d(24)]
    plan += [h(2, s) for s in range(n)]
    return tuple(plan)


def fused_scratch(n_node, experts, tok, width, ff, top):
    half = tok // 2
    heights = (tok, half, half)
    bf16 = jnp.bfloat16
    held = tok * 2 * experts // LANES
    most = 2 * CORES * tok
    items = len(heights)

    def each(*lead):
        return [(lead + (height, width), bf16) for height in heights]

    buffers = [
        ((items, n_node, 2, CORES, tok, width), bf16),
        ((n_node, 2, CORES, held, LANES), jnp.float32),
        ((2, tok, top), jnp.int32),
        ((2, tok, top), jnp.float32),
        ((width, ff), bf16),
        ((width, ff), bf16),
        ((ff, width), bf16),
        ((most, ff), bf16),
        ((most, ff), bf16),
    ]
    buffers += each(n_node, 2, CORES) + each(n_node, 2) + each(n_node) + each(2, n_node) + each()
    semaphores = [
        (12,),
        (items + 1, n_node + 1, 2),
        (items + 1, n_node, 2),
        (items + 1, n_node),
        (items + 1, n_node),
        (items + 1, n_node, 2),
        (items + 1, n_node, 2),
        (items, n_node, 2),
        (items, n_node, 2),
        (items, n_node),
        (items, n_node),
        (items, n_node),
        (items, 2, n_node),
        (items,),
        (items,),
    ]
    return buffers, semaphores


def fits(n_node, n_x, experts, tok, width, ff, top):
    if n_x != 2 or n_node < 3 or tok % (4 * ROW_TILE) or ff % 256 or width % 512:
        return False
    if LANES % (2 * experts) or tok % (LANES // (2 * experts)):
        return False
    held = tok * 2 * experts // LANES
    if held % 8 or (tok // 2) % held:
        return False
    buffers, _ = fused_scratch(n_node, experts, tok, width, ff, top)
    return sum(math.prod(shape) * jnp.dtype(kind).itemsize for shape, kind in buffers) < VMEM_BYTES * 7 // 8


def fused(arrays, n_section, n_node, experts):
    tok, width = arrays[0].shape
    top, ff = arrays[1].shape[1], arrays[7].shape[1]
    buffers, semaphores = fused_scratch(n_node, experts, tok, width, ff, top)
    shape = (n_section, n_node, experts, tok, tok // 4, schedule(n_node))
    return pl.pallas_call(
        functools.partial(fused_kernel, shape),
        out_shape=[jax.ShapeDtypeStruct((tok, width), jnp.bfloat16)] * 2,
        in_specs=[pl.BlockSpec(memory_space=pl.ANY)] * len(arrays),
        out_specs=[pl.BlockSpec(memory_space=pl.ANY)] * 2,
        scratch_shapes=[pltpu.VMEM(*buffer) for buffer in buffers]
        + [pltpu.SemaphoreType.DMA(count) for count in semaphores],
        compiler_params=pltpu.CompilerParams(
            collective_id=2, has_side_effects=True, vmem_limit_bytes=67043328
        ),
    )(*arrays)


def local(
    forward_input,
    forward_routes,
    forward_gates,
    backward_input,
    backward_cotangent,
    backward_routes,
    backward_gates,
    w_gate,
    w_up,
    w_down,
):
    experts = lax.axis_size("node") * lax.axis_size("lane") * w_gate.shape[1]
    w_g, w_u, w_d = w_gate[0, 0], w_up[0, 0], w_down[0, 0]
    n_node, n_x = lax.axis_size("node"), lax.axis_size("lane") // CORES
    tok, width, top, ff = *forward_input.shape[1:], forward_routes.shape[2], w_g.shape[1]
    if w_gate.shape[1] == 1 and fits(n_node, n_x, experts, tok, width, ff, top):
        mine = (forward_input[0], forward_routes[0], forward_gates[0], backward_input[0],
                backward_cotangent[0], backward_routes[0], backward_gates[0], w_g, w_u, w_d)
        outs = fused(mine, lax.axis_size("section"), n_node, experts)
        return (outs[0][None], outs[1][None])
    me = lax.axis_index(GROUP)

    coef = jnp.concatenate(
        [
            coefficients(forward_routes[0], forward_gates[0], experts),
            coefficients(backward_routes[0], backward_gates[0], experts),
        ],
        axis=1,
    )
    coef = jnp.pad(coef, ((0, 0), (0, -coef.shape[1] % 128)))
    tokens = forward_input.shape[1] * lax.axis_size("node") * lax.axis_size("lane")
    coef, fwd, bwd, cot = (
        array.reshape(tokens, -1)
        for array in gather(coef, forward_input[0], backward_input[0], backward_cotangent[0])
    )
    fwd_coef = lax.dynamic_slice_in_dim(coef, me, 1, axis=1)
    bwd_coef = lax.dynamic_slice_in_dim(coef, experts + me, 1, axis=1)

    pre_gate = jnp.dot(fwd, w_g, preferred_element_type=jnp.float32)
    pre_up = jnp.dot(fwd, w_u, preferred_element_type=jnp.float32)
    hidden = (jax.nn.silu(pre_gate) * pre_up).astype(jnp.bfloat16)
    hidden = lax.optimization_barrier(hidden)
    out = jnp.dot(hidden, w_d, preferred_element_type=jnp.float32)
    out = (out * fwd_coef).astype(jnp.bfloat16)

    pre_gate = jnp.dot(bwd, w_g, preferred_element_type=jnp.float32)
    pre_up = jnp.dot(bwd, w_u, preferred_element_type=jnp.float32)
    grad_hidden = contract_last(cot, w_d) * bwd_coef
    sigma = jax.nn.sigmoid(pre_gate)
    grad_gate = (grad_hidden * pre_up * sigma * (1.0 + pre_gate * (1.0 - sigma))).astype(
        jnp.bfloat16
    )
    grad_up = (grad_hidden * pre_gate * sigma).astype(jnp.bfloat16)
    grad_gate, grad_up = lax.optimization_barrier((grad_gate, grad_up))
    total = contract_last(grad_gate, w_g) + contract_last(grad_up, w_u)
    next_input, previous_gradient = scatter(out, total.astype(jnp.bfloat16))
    return (next_input[None], previous_gradient[None])


def solution(mesh):
    rows = P("section", GROUP, None)
    weights = P("section", GROUP, None, None)
    return jax.shard_map(
        local,
        mesh=mesh,
        in_specs=(rows,) * 7 + (weights,) * 3,
        out_specs=(rows, rows),
        check_vma=False,
    )
```

```python
import functools
import math

import jax
import jax.numpy as jnp
from jax import lax
from jax.experimental import pallas as pl
from jax.experimental.pallas import tpu as pltpu
from jax.sharding import PartitionSpec as P

GROUP = ("node", "lane")
CORES = 2
MESH = pl.DeviceIdType.MESH


def position():
    node, lane = lax.axis_index("node"), lax.axis_index("lane")
    return node, lane // CORES, lane % CORES


def greet(peers):
    barrier = pltpu.get_barrier_semaphore()
    for cond, device in peers:
        @pl.when(cond)
        def _():
            pl.semaphore_signal(barrier, inc=1, device_id=device, device_id_type=MESH)
    pl.semaphore_wait(barrier, sum(jnp.where(cond, 1, 0) for cond, _ in peers))


def gather_kernel(n_node, n_x, count, *refs):
    ins, outs = refs[:count], refs[count : 2 * count]
    local_sem, recv, z_sem, x_sem, core_sem = refs[2 * count :]
    node, x, core = position()
    lane = x * CORES + core
    z_up, z_down = {"node": node + 1}, {"node": node - 1}
    x_up, x_down = {"lane": lane + CORES}, {"lane": lane - CORES}
    partner = {"lane": lane + 1 - 2 * core}
    has_up, has_down = node < n_node - 1, node > 0
    has_right, has_left = x < n_x - 1, x > 0
    greet(
        [
            (has_up, z_up),
            (has_down, z_down),
            (has_right, x_up),
            (has_left, x_down),
            (core < CORES, partner),
        ]
    )
    sends = []

    def send(cond, a, src, z, at_x, sem, device):
        where = outs[a].at[z, at_x * CORES + core]

        def copy():
            return pltpu.make_async_remote_copy(
                src_ref=where if src is None else src,
                dst_ref=where,
                send_sem=sem,
                recv_sem=recv.at[a, z, at_x * CORES + core],
                device_id=device,
                device_id_type=MESH,
            )

        @pl.when(cond)
        def _():
            copy().start()

        sends.append((cond, copy))

    def arrived(a, z, at_lane):
        where = outs[a].at[z, at_lane]
        pltpu.make_async_remote_copy(
            src_ref=where,
            dst_ref=where,
            send_sem=core_sem.at[a, 0, 0],
            recv_sem=recv.at[a, z, at_lane],
            device_id=partner,
            device_id_type=MESH,
        ).wait_recv()

    def along_x(cond, a, src, z):
        send(cond & has_right, a, src, z, x, x_sem.at[a, 0, z, x], x_up)
        send(cond & has_left, a, src, z, x, x_sem.at[a, 1, z, x], x_down)
        send(cond, a, src, z, x, core_sem.at[a, z, x], partner)

    always = core < CORES
    keeps = []
    for a in range(count):
        send(has_up, a, ins[a], node, x, z_sem.at[a, 0, node], z_up)
        send(has_down, a, ins[a], node, x, z_sem.at[a, 1, node], z_down)
        along_x(always, a, ins[a], node)
    for a in range(count):
        keep = pltpu.make_async_copy(ins[a], outs[a].at[node, lane], local_sem.at[a])
        keep.start()
        keeps.append(keep)
    for step in range(1, n_node):
        for a in range(count):
            below, above = node - step, node + step
            from_below, from_above = below >= 0, above < n_node

            @pl.when(from_below)
            def _():
                arrived(a, below, lane)

            send(from_below & has_up, a, None, below, x, z_sem.at[a, 0, below], z_up)
            along_x(from_below, a, None, below)

            @pl.when(from_above)
            def _():
                arrived(a, above, lane)

            send(from_above & has_down, a, None, above, x, z_sem.at[a, 1, above], z_down)
            along_x(from_above, a, None, above)
    for step in range(1, n_x):
        for a in range(count):
            for k in range(n_node):
                z = (node + k) % n_node
                for at_x, cond, go_on, way, device in (
                    (x - step, x - step >= 0, has_right, 0, x_up),
                    (x + step, x + step < n_x, has_left, 1, x_down),
                ):
                    @pl.when(cond)
                    def _():
                        arrived(a, z, at_x * CORES + core)

                    if n_x > 2:
                        send(cond & go_on, a, None, z, at_x, x_sem.at[a, way, z, at_x], device)
                    send(cond, a, None, z, at_x, core_sem.at[a, z, at_x], partner)
    for a in range(count):
        for k in range(n_node):
            for at_x in range(n_x):
                arrived(a, k, at_x * CORES + 1 - core)
    for cond, copy in sends:
        @pl.when(cond)
        def _():
            copy().wait_send()
    for keep in keeps:
        keep.wait()


def gather(*arrays):
    n_node, n_lane = lax.axis_size("node"), lax.axis_size("lane")
    n_x, count = n_lane // CORES, len(arrays)
    return pl.pallas_call(
        functools.partial(gather_kernel, n_node, n_x, count),
        out_shape=[jax.ShapeDtypeStruct((n_node, n_lane) + a.shape, a.dtype) for a in arrays],
        in_specs=[pl.BlockSpec(memory_space=pltpu.VMEM)] * count,
        out_specs=[pl.BlockSpec(memory_space=pl.ANY)] * count,
        scratch_shapes=[
            pltpu.SemaphoreType.DMA((count,)),
            pltpu.SemaphoreType.DMA((count, n_node, n_lane)),
            pltpu.SemaphoreType.DMA((count, 2, n_node)),
            pltpu.SemaphoreType.DMA((count, 2, n_node, n_x)),
            pltpu.SemaphoreType.DMA((count, n_node, n_x)),
        ],
        compiler_params=pltpu.CompilerParams(collective_id=0, has_side_effects=True),
    )(*arrays)


def scatter_kernel(n_section, n_node, n_x, count, *refs):
    parts, outs = refs[:count], refs[count : 2 * count]
    (own, core_in, x_in, z_in, final, local_sem, core_send, core_recv, x_send, x_recv, z_send,
     z_recv, y_send, y_recv) = refs[2 * count :]
    node, x, core = position()
    section = lax.axis_index("section")
    lane = x * CORES + core
    partner = {"lane": lane + 1 - 2 * core}
    z_up, z_down = {"node": node + 1}, {"node": node - 1}
    x_up, x_down = {"lane": lane + CORES}, {"lane": lane - CORES}
    after = {"section": (section + 1) % n_section}
    before = {"section": (section + n_section - 1) % n_section}
    has_up, has_down = node < n_node - 1, node > 0
    has_right, has_left = x < n_x - 1, x > 0
    always = core < CORES
    greet(
        [
            (has_up, z_up),
            (has_down, z_down),
            (has_right, x_up),
            (has_left, x_down),
            (always, partner),
            (always, after),
            (always, before),
        ]
    )

    def remote(src, dst, send_sem, recv_sem, device):
        return pltpu.make_async_remote_copy(
            src_ref=src,
            dst_ref=dst,
            send_sem=send_sem,
            recv_sem=recv_sem,
            device_id=device,
            device_id_type=MESH,
        )

    def add(target, *others):
        total = target[...].astype(jnp.float32)
        for other in others:
            total = total + other[...].astype(jnp.float32)
        target[...] = total.astype(target.dtype)

    sends = []

    def start(cond, make):
        @pl.when(cond)
        def _():
            make().start()

        sends.append((cond, make))

    owners = []
    for t in range(n_node - 1):
        owners.append((node + n_node - 1 - t, t >= node))
        owners.append((t + node - (n_node - 1), t + node >= n_node - 1))
    x_steps = [
        (t, x + n_x - 1 - t, t >= x, t + x - (n_x - 1), t + x >= n_x - 1) for t in range(n_x - 1)
    ]
    every = owners + [(node, always)]

    loads = []
    for a in range(count):
        load = pltpu.make_async_copy(parts[a].at[:, :, core], own.at[a], local_sem.at[a])
        load.start()
        loads.append(load)

    def core_copy(a, z, at_x):
        return remote(
            parts[a].at[z, at_x, 1 - core],
            core_in.at[a, z, at_x],
            core_send.at[a, z, at_x],
            core_recv.at[a, z, at_x],
            partner,
        )

    for a in range(count):
        for z, cond in every:
            for _, q_up, c_up, q_down, c_down in x_steps:
                start(cond & c_up, functools.partial(core_copy, a, z, q_up))
                start(cond & c_down, functools.partial(core_copy, a, z, q_down))
        for z, cond in every:
            start(cond, functools.partial(core_copy, a, z, x))

    def x_copy(a, z, q, slot, device):
        return remote(
            own.at[a, z, q], x_in.at[a, z, slot], x_send.at[a, z, q], x_recv.at[a, z, slot], device
        )

    def z_copy(a, z, slot, device):
        return remote(
            own.at[a, z, x], z_in.at[a, slot], z_send.at[a, z], z_recv.at[a, slot], device
        )

    for a in range(count):
        loads[a].wait()
        for z, cond in every:
            for t, q_up, c_up, q_down, c_down in x_steps:
                for q, c, more, slot, device in (
                    (q_up, c_up, has_left, q_up, x_up),
                    (q_down, c_down, has_right, None, x_down),
                ):
                    @pl.when(cond & c)
                    def _():
                        core_copy(a, z, q).wait_recv()
                        add(own.at[a, z, q], core_in.at[a, z, q])

                    if t > 0:
                        @pl.when(cond & c & more)
                        def _():
                            x_copy(a, z, q, q, partner).wait_recv()
                            add(own.at[a, z, q], x_in.at[a, z, q])

                    if slot is not None:
                        start(cond & c, functools.partial(x_copy, a, z, q, slot, device))
                    else:
                        near = q == x - 1
                        start(
                            cond & c & near, functools.partial(x_copy, a, z, q, n_x, device)
                        )
                        if n_x > 2:
                            start(
                                cond & c & (q < x - 1),
                                functools.partial(x_copy, a, z, q, q, device),
                            )

    def collect(a, z):
        core_copy(a, z, x).wait_recv()
        add(own.at[a, z, x], core_in.at[a, z, x])
        for c, slot in ((has_left, x), (has_right, n_x)):
            @pl.when(c)
            def _():
                x_copy(a, z, 0, slot, partner).wait_recv()
                add(own.at[a, z, x], x_in.at[a, z, slot])

    for a in range(count):
        for k, (z, cond) in enumerate(owners):
            going_up = k % 2 == 0

            @pl.when(cond)
            def _():
                collect(a, z)

            if k >= 2:
                @pl.when(cond & (has_down if going_up else has_up))
                def _():
                    z_copy(a, z, z, partner).wait_recv()
                    add(own.at[a, z, x], z_in.at[a, z])

            if going_up:
                start(cond, functools.partial(z_copy, a, z, z, z_up))
            else:
                start(cond & (z == node - 1), functools.partial(z_copy, a, z, n_node, z_down))
                if n_node > 2:
                    start(cond & (z < node - 1), functools.partial(z_copy, a, z, z, z_down))
        collect(a, node)

    def y_copy(a):
        return remote(
            final.at[a], outs[a], y_send.at[a], y_recv.at[a], after if a == 0 else before
        )

    for a in range(count):
        for c, slot in ((has_down, node), (has_up, n_node)):
            @pl.when(c)
            def _():
                z_copy(a, node, slot, partner).wait_recv()
                add(own.at[a, node, x], z_in.at[a, slot])
        final[a] = own[a, node, x]
        y_copy(a).start()
    for a in range(count):
        y_copy(a).wait()
    for cond, make in sends:
        @pl.when(cond)
        def _():
            make().wait_send()


def scatter(*parts):
    n_section, n_node = lax.axis_size("section"), lax.axis_size("node")
    n_x, count = lax.axis_size("lane") // CORES, len(parts)
    rows, width = parts[0].shape
    tok = rows // (n_node * n_x * CORES)
    dtype = parts[0].dtype
    block = (tok, width)
    dma = pltpu.SemaphoreType.DMA
    return pl.pallas_call(
        functools.partial(scatter_kernel, n_section, n_node, n_x, count),
        out_shape=[jax.ShapeDtypeStruct(block, dtype)] * count,
        in_specs=[pl.BlockSpec(memory_space=pl.ANY)] * count,
        out_specs=[pl.BlockSpec(memory_space=pltpu.VMEM)] * count,
        scratch_shapes=[
            pltpu.VMEM((count, n_node, n_x) + block, dtype),
            pltpu.VMEM((count, n_node, n_x) + block, dtype),
            pltpu.VMEM((count, n_node, n_x + 1) + block, dtype),
            pltpu.VMEM((count, n_node + 1) + block, dtype),
            pltpu.VMEM((count,) + block, dtype),
            dma((count,)),
            dma((count, n_node, n_x)),
            dma((count, n_node, n_x)),
            dma((count, n_node, n_x)),
            dma((count, n_node, n_x + 1)),
            dma((count, n_node)),
            dma((count, n_node + 1)),
            dma((count,)),
            dma((count,)),
        ],
        compiler_params=pltpu.CompilerParams(
            collective_id=1, has_side_effects=True, vmem_limit_bytes=67043328
        ),
    )(*(part.reshape((n_node, n_x, CORES) + block) for part in parts))


def coefficients(routes, gates, experts):
    hit = routes[:, :, None] == jnp.arange(experts, dtype=jnp.int32)[None, None, :]
    return jnp.sum(jnp.where(hit, gates[:, :, None], 0.0), axis=1)


def contract_last(a, b):
    return lax.dot_general(a, b, (((1,), (1,)), ((), ())), preferred_element_type=jnp.float32)


VMEM_BYTES = 64 * 2**20
ROW_TILE = 16
LANES = 128


def distance_order(n):
    return [sorted(range(n), key=lambda other: (abs(other - z), (z >= n // 2) != (other > z))) for z in range(n)]


def fused_kernel(shape, *refs):
    n_section, n_node, experts, tok, cross, plan = shape
    (f_in, f_routes, f_gates, b_in, cot_in, b_routes, b_gates, wg_in, wu_in, wd_in) = refs[:10]
    outs = refs[10:12]
    (rows, coefs, routes, gates, w_g, w_u, w_d, w_gt, w_ut, w_dt, hid_a, hid_b) = refs[12:24]
    n_items = 3
    parts, core_in, x_in, z_in, last = (refs[24 + n_items * k : 24 + n_items * (k + 1)] for k in range(5))
    (ls, zs, zr, xs, xr, cs, cr, es, er, rs, rr, hs, hr, ys, yr) = refs[24 + 5 * n_items :]
    half = tok // 2
    node, x, core = position()
    section = lax.axis_index("section")
    lane = x * CORES + core
    me = node * (2 * CORES) + lane
    z_up, z_down = {"node": node + 1}, {"node": node - 1}
    beside = {"lane": (1 - x) * CORES + core}
    partner = {"lane": lane + 1 - 2 * core}
    after = {"section": (section + 1) % n_section}
    before = {"section": (section + n_section - 1) % n_section}
    has_up, has_down = node < n_node - 1, node > 0
    always = core < CORES
    order = distance_order(n_node)

    def near(k):
        found = order[0][k]
        for z in range(1, n_node):
            found = jnp.where(node == z, order[z][k], found)
        return found

    loads = []

    def load(src, dst):
        loads.append(pltpu.make_async_copy(src, dst, ls.at[len(loads)]))
        loads[-1].start()
        return loads[-1]

    small = [
        load(f_routes, routes.at[0]),
        load(b_routes, routes.at[1]),
        load(f_gates, gates.at[0]),
        load(b_gates, gates.at[1]),
    ]
    own = [[load(f_in, rows.at[0, node, x, core])]]
    for h in range(2):
        own.append(
            [
                load(b_in.at[pl.ds(h * half, half)], rows.at[1 + h, node, x, core, pl.ds(0, half)]),
                load(cot_in.at[pl.ds(h * half, half)], rows.at[1 + h, node, x, core, pl.ds(half, half)]),
            ]
        )
    weights = [load(wg_in, w_g), load(wu_in, w_u), load(wd_in, w_d)]

    for copy in small:
        copy.wait()
    groups = LANES // (2 * experts)
    held = tok // groups
    top = routes.shape[1]
    lists = [routes[0].astype(jnp.float32), routes[1].astype(jnp.float32), gates[0], gates[1]]
    lists = jnp.concatenate(lists, axis=0)
    lists = jnp.concatenate([lists, jnp.zeros((4 * top, LANES - tok), jnp.float32)], axis=1)
    lists = jnp.concatenate([lists, jnp.zeros((LANES - 4 * top, LANES), jnp.float32)], axis=0).T
    at = lax.broadcasted_iota(jnp.int32, (held, LANES), 1).astype(jnp.float32)
    packed = jnp.zeros((held, LANES), jnp.float32)
    for which in range(2):
        for g in range(groups):
            some = lists[g * held : (g + 1) * held]
            for k in range(top):
                slot = which * top + k
                chosen = at == some[:, slot : slot + 1] + float((g * 2 + which) * experts)
                packed = packed + jnp.where(chosen, some[:, 2 * top + slot : 2 * top + slot + 1], 0.0)
    coefs[node, x, core] = packed

    greet(
        [
            (has_up, z_up),
            (has_down, z_down),
            (always, beside),
            (always, partner),
            (always, after),
            (always, before),
        ]
    )

    pending = []

    def remote(src, dst, send_sem, recv_sem, device):
        return pltpu.make_async_remote_copy(
            src_ref=src, dst_ref=dst, send_sem=send_sem, recv_sem=recv_sem,
            device_id=device, device_id_type=MESH,
        )

    def start(cond, make):
        if cond is None:
            make().start()
        else:
            @pl.when(cond)
            def _():
                make().start()
        pending.append((cond, make))

    def drain(keep=0):
        while len(pending) > keep:
            cond, make = pending.pop(0)
            if cond is None:
                make().wait_send()
            else:
                @pl.when(cond)
                def _():
                    make().wait_send()

    n_coef = n_items
    T1 = pl.ds(0, tok - cross)
    T2 = pl.ds(tok - cross, cross)

    def block(i, z, at_x, at_core=None):
        at_core = core if at_core is None else at_core
        return coefs.at[z, at_x, at_core] if i == n_coef else rows.at[i, z, at_x, at_core]

    def z_piece(i, z, p):
        return rows.at[i, z, 1 - x, core, T2] if p else block(i, z, x)

    def x_piece(i, z, at_x, whole):
        return block(i, z, at_x) if whole or i == n_coef else rows.at[i, z, at_x, core, T1]

    def z_copy(i, z, p, slot, device):
        where = z_piece(i, z, p)
        return remote(where, where, zs.at[i, slot, p], zr.at[i, z, p], device)

    def x_copy(i, z, at_x, whole):
        where = x_piece(i, z, at_x, whole)
        return remote(where, where, xs.at[i, z], xr.at[i, z], beside)

    def c_copy(i, z, at_x, at_core, q):
        where = block(i, z, at_x, at_core)
        return remote(where, where, cs.at[i, z, q], cr.at[i, z, q], partner)

    both = functools.partial

    def along_z(i, z, p):
        start(has_up, both(z_copy, i, z, p, z, z_up))
        start(has_down, both(z_copy, i, z, p, n_node, z_down))

    def members(i):
        return (n_coef, i) if i == 0 else (i,)

    def sides(j):
        return (
            (node - j, node - j >= 0, has_up, z_up),
            (node + j, node + j < n_node, has_down, z_down),
        )

    def arrive_z(i, j):
        if j == 0:
            for copy in own[i]:
                copy.wait()
            for m in members(i):
                along_z(m, node, 0)
                start(None, both(x_copy, m, node, x, True))
                start(None, both(c_copy, m, node, x, core, 0))
            return
        for z, there, go, device in sides(j):
            for m in members(i):
                @pl.when(there)
                def _():
                    z_copy(m, z, 0, z, device).wait_recv()

                start(there & go, both(z_copy, m, z, 0, z, device))
                start(there, both(x_copy, m, z, x, False))
                start(there, both(c_copy, m, z, x, core, 0))

    def relay_other(i, j):
        for z, there, go, device in sides(j):
            @pl.when(there)
            def _():
                z_copy(i, z, 1, z, device).wait_recv()

            start(there & go, both(z_copy, i, z, 1, z, device))

    def arrive_x(i, j):
        if j == 0:
            for m in members(i):
                x_copy(m, node, 1 - x, True).wait_recv()
                if m != n_coef:
                    along_z(m, node, 1)
                start(None, both(c_copy, m, node, 1 - x, core, 1))
            return
        for z, there, _, _ in sides(j):
            for m in members(i):
                @pl.when(there)
                def _():
                    x_copy(m, z, 1 - x, False).wait_recv()

                start(there, both(c_copy, m, z, 1 - x, core, 1))

    def exchange(i, z, at_x):
        return remote(
            parts[i].at[z, at_x, 1 - core], core_in[i].at[z, at_x],
            es.at[i, z, at_x], er.at[i, z, at_x], partner,
        )

    def coef_of(z, which, first, count):
        where = lax.broadcasted_iota(jnp.int32, (held, LANES), 1)
        columns = []
        for at_x in range(2):
            for at_core in range(CORES):
                values = coefs[z, at_x, at_core]
                for g in range(first // held, (first + count) // held):
                    wanted = where == g * (2 * experts) + which * experts + me
                    columns.append(jnp.sum(jnp.where(wanted, values, 0.0), axis=1, keepdims=True))
        return jnp.concatenate(columns, axis=0)

    ff, width = w_d.shape
    wide = width // 2

    def turn():
        for copy in weights:
            copy.wait()

        @pl.loop(0, width // 256)
        def _(j):
            js = pl.ds(pl.multiple_of(j * 256, 256), 256)
            w_gt[:, js] = w_g[js, :].T
            w_ut[:, js] = w_u[js, :].T
            w_dt[js, :] = w_d[:, js].T

    def forward(z):
        count = 2 * CORES * tok
        coef = coef_of(z, 0, 0, tok)
        v = rows[0, z].reshape(count, width)
        a = jnp.dot(v, w_g[...], preferred_element_type=jnp.float32)
        b = jnp.dot(v, w_u[...], preferred_element_type=jnp.float32)
        hid_a[...] = (a / (1.0 + jnp.exp(-a)) * b).astype(jnp.bfloat16)

        @pl.loop(0, width // wide)
        def _(j):
            js = pl.ds(pl.multiple_of(j * wide, wide), wide)
            out = jnp.dot(hid_a[...], w_d[:, js], preferred_element_type=jnp.float32) * coef
            parts[0][z, :, :, :, js] = out.astype(jnp.bfloat16).reshape(2, CORES, tok, wide)

    def backward(i, z):
        count = 2 * CORES * half
        coef = coef_of(z, 1, (i - 1) * half, half)
        v = rows[i, z, :, :, 0:half].reshape(count, width)
        g = rows[i, z, :, :, half:].reshape(count, width)
        a = jnp.dot(v, w_g[...], preferred_element_type=jnp.float32)
        b = jnp.dot(v, w_u[...], preferred_element_type=jnp.float32)
        h = jnp.dot(g, w_dt[...], preferred_element_type=jnp.float32) * coef
        q = 1.0 / (1.0 + jnp.exp(-a))
        hid_a[0:count] = (h * b * q * (1.0 + a * (1.0 - q))).astype(jnp.bfloat16)
        hid_b[0:count] = (h * a * q).astype(jnp.bfloat16)

        @pl.loop(0, width // wide)
        def _(j):
            js = pl.ds(pl.multiple_of(j * wide, wide), wide)
            total = jnp.dot(hid_a[0:count], w_gt[:, js], preferred_element_type=jnp.float32)
            total = total + jnp.dot(hid_b[0:count], w_ut[:, js], preferred_element_type=jnp.float32)
            parts[i][z, :, :, :, js] = total.astype(jnp.bfloat16).reshape(2, CORES, half, wide)

    def compute(i, k):
        z = near(k)
        for m in members(i):
            c_copy(m, z, x, 1 - core, 0).wait_recv()
            c_copy(m, z, 1 - x, 1 - core, 1).wait_recv()
        forward(z) if i == 0 else backward(i, z)
        for at_x in (1 - x, x):
            start(None, both(exchange, i, z, at_x))

    def total_of(*terms):
        total = terms[0].astype(jnp.float32)
        for term in terms[1:]:
            total = total + term.astype(jnp.float32)
        return total.astype(jnp.bfloat16)

    def r_copy(i, z):
        return remote(parts[i].at[z, 1 - x, core], x_in[i].at[z], rs.at[i, z], rr.at[i, z], beside)

    def cross_x(i, k):
        z = near(k)
        exchange(i, z, 1 - x).wait_recv()
        parts[i][z, 1 - x, core] = total_of(parts[i][z, 1 - x, core], core_in[i][z, 1 - x])
        start(None, both(r_copy, i, z))

    def h_copy(i, z, way):
        return remote(
            parts[i].at[z, x, core], z_in[i].at[way, z], hs.at[i, z], hr.at[i, way, z],
            (z_up, z_down)[way],
        )

    def y_copy(i):
        a = 0 if i == 0 else 1
        dst = outs[0] if i == 0 else outs[1].at[pl.ds((i - 1) * half, half)]
        return remote(last[i], dst, ys.at[i], yr.at[i], after if a == 0 else before)

    def chain(i, s):
        if s == n_node - 1:
            exchange(i, node, x).wait_recv()
            r_copy(i, node).wait_recv()
            for ways, there in (((0,), node == n_node - 1), ((1,), node == 0), ((0, 1), has_down & has_up)):
                @pl.when(there)
                def _():
                    for way in ways:
                        h_copy(i, node, way).wait_recv()
                    arrived = [z_in[i][way, node] for way in ways]
                    terms = [parts[i][node, x, core], core_in[i][node, x], x_in[i][node]]
                    last[i][...] = total_of(*terms, *arrived)

            y_copy(i).start()
            return
        for way, z, there, more in (
            (0, n_node - 1 + node - s, s >= node, has_down),
            (1, s + node - (n_node - 1), s + node >= n_node - 1, has_up),
        ):
            @pl.when(there)
            def _():
                exchange(i, z, x).wait_recv()
                r_copy(i, z).wait_recv()

            def mine():
                return [parts[i][z, x, core], core_in[i][z, x], x_in[i][z]]

            @pl.when(there & more)
            def _():
                h_copy(i, z, way).wait_recv()
                parts[i][z, x, core] = total_of(*mine(), z_in[i][way, z])

            @pl.when(there & (node == (n_node - 1) * way))
            def _():
                parts[i][z, x, core] = total_of(*mine())

            start(there, both(h_copy, i, z, way))

    for step in plan:
        kind, i, k = step
        if kind == "D":
            drain(k)
        elif kind == "W":
            turn()
        else:
            {"A": arrive_z, "T": relay_other, "X": arrive_x, "C": compute, "R": cross_x, "H": chain}[kind](i, k)
    for i in range(n_items):
        y_copy(i).wait()
    drain()


ORDER = (
    "A00 A10 W00 X00",
    "A01 C00 A11 T01",
    "X01 R00 C01 R01",
    "X10 A02 T02 A12",
    "C10 T11 X11 A20",
    "C11 R10 X02 A03",
    "C02 R02 X20 T03",
    "A13 X03 C03 T12",
    "X12 R03 C20 A21",
    "C12 T13 R11 R12",
    "X13 H00 C13 A22",
    "T21 H01 R20 X21",
    "C21 A23 T22 X22",
    "R13 H02 C22 T23",
    "X23 R21 R22 H10",
    "C23 H11 R23 H12",
    "H20 H03 H21 H22",
    "H13 H23",
)


def schedule():
    steps = [step for line in ORDER for step in line.split()]
    return tuple((step[0], int(step[1]), int(step[2:])) for step in steps)


def fused_scratch(n_node, experts, tok, width, ff, top):
    half = tok // 2
    heights = (tok, half, half)
    bf16 = jnp.bfloat16
    held = tok * 2 * experts // LANES
    most = 2 * CORES * tok
    items = len(heights)

    def each(*lead):
        return [(lead + (height, width), bf16) for height in heights]

    buffers = [
        ((items, n_node, 2, CORES, tok, width), bf16),
        ((n_node, 2, CORES, held, LANES), jnp.float32),
        ((2, top, tok), jnp.int32),
        ((2, top, tok), jnp.float32),
        ((width, ff), bf16),
        ((width, ff), bf16),
        ((ff, width), bf16),
        ((ff, width), bf16),
        ((ff, width), bf16),
        ((width, ff), bf16),
        ((most, ff), bf16),
        ((most, ff), bf16),
    ]
    buffers += each(n_node, 2, CORES) + each(n_node, 2) + each(n_node) + each(2, n_node) + each()
    semaphores = [
        (12,),
        (items + 1, n_node + 1, 2),
        (items + 1, n_node, 2),
        (items + 1, n_node),
        (items + 1, n_node),
        (items + 1, n_node, 2),
        (items + 1, n_node, 2),
        (items, n_node, 2),
        (items, n_node, 2),
        (items, n_node),
        (items, n_node),
        (items, n_node),
        (items, 2, n_node),
        (items,),
        (items,),
    ]
    return buffers, semaphores


def fits(n_node, n_x, experts, tok, width, ff, top):
    if n_x != 2 or n_node != 4 or tok % (4 * ROW_TILE) or ff % 256 or width % 512:
        return False
    if LANES % (2 * experts) or tok % (LANES // (2 * experts)):
        return False
    held = tok * 2 * experts // LANES
    if held % 8 or (tok // 2) % held or tok > LANES or 4 * top > LANES:
        return False
    buffers, _ = fused_scratch(n_node, experts, tok, width, ff, top)
    return sum(math.prod(shape) * jnp.dtype(kind).itemsize for shape, kind in buffers) < VMEM_BYTES * 7 // 8


def fused(arrays, n_section, n_node, experts):
    tok, width = arrays[0].shape
    top, ff = arrays[1].shape[0], arrays[7].shape[1]
    buffers, semaphores = fused_scratch(n_node, experts, tok, width, ff, top)
    shape = (n_section, n_node, experts, tok, tok // 2, schedule())
    return pl.pallas_call(
        functools.partial(fused_kernel, shape),
        out_shape=[jax.ShapeDtypeStruct((tok, width), jnp.bfloat16)] * 2,
        in_specs=[pl.BlockSpec(memory_space=pl.ANY)] * len(arrays),
        out_specs=[pl.BlockSpec(memory_space=pl.ANY)] * 2,
        scratch_shapes=[pltpu.VMEM(*buffer) for buffer in buffers]
        + [pltpu.SemaphoreType.DMA(count) for count in semaphores],
        compiler_params=pltpu.CompilerParams(
            collective_id=2, has_side_effects=True, vmem_limit_bytes=67043328
        ),
    )(*arrays)


def local(
    forward_input,
    forward_routes,
    forward_gates,
    backward_input,
    backward_cotangent,
    backward_routes,
    backward_gates,
    w_gate,
    w_up,
    w_down,
):
    experts = lax.axis_size("node") * lax.axis_size("lane") * w_gate.shape[1]
    w_g, w_u, w_d = w_gate[0, 0], w_up[0, 0], w_down[0, 0]
    n_node, n_x = lax.axis_size("node"), lax.axis_size("lane") // CORES
    tok, width, top, ff = *forward_input.shape[1:], forward_routes.shape[2], w_g.shape[1]
    if w_gate.shape[1] == 1 and fits(n_node, n_x, experts, tok, width, ff, top):
        mine = (forward_input[0], forward_routes[0].T, forward_gates[0].T, backward_input[0],
                backward_cotangent[0], backward_routes[0].T, backward_gates[0].T, w_g, w_u, w_d)
        outs = fused(mine, lax.axis_size("section"), n_node, experts)
        return (outs[0][None], outs[1][None])
    me = lax.axis_index(GROUP)

    coef = jnp.concatenate(
        [
            coefficients(forward_routes[0], forward_gates[0], experts),
            coefficients(backward_routes[0], backward_gates[0], experts),
        ],
        axis=1,
    )
    coef = jnp.pad(coef, ((0, 0), (0, -coef.shape[1] % 128)))
    tokens = forward_input.shape[1] * lax.axis_size("node") * lax.axis_size("lane")
    coef, fwd, bwd, cot = (
        array.reshape(tokens, -1)
        for array in gather(coef, forward_input[0], backward_input[0], backward_cotangent[0])
    )
    fwd_coef = lax.dynamic_slice_in_dim(coef, me, 1, axis=1)
    bwd_coef = lax.dynamic_slice_in_dim(coef, experts + me, 1, axis=1)

    pre_gate = jnp.dot(fwd, w_g, preferred_element_type=jnp.float32)
    pre_up = jnp.dot(fwd, w_u, preferred_element_type=jnp.float32)
    hidden = (jax.nn.silu(pre_gate) * pre_up).astype(jnp.bfloat16)
    hidden = lax.optimization_barrier(hidden)
    out = jnp.dot(hidden, w_d, preferred_element_type=jnp.float32)
    out = (out * fwd_coef).astype(jnp.bfloat16)

    pre_gate = jnp.dot(bwd, w_g, preferred_element_type=jnp.float32)
    pre_up = jnp.dot(bwd, w_u, preferred_element_type=jnp.float32)
    grad_hidden = contract_last(cot, w_d) * bwd_coef
    sigma = jax.nn.sigmoid(pre_gate)
    grad_gate = (grad_hidden * pre_up * sigma * (1.0 + pre_gate * (1.0 - sigma))).astype(
        jnp.bfloat16
    )
    grad_up = (grad_hidden * pre_gate * sigma).astype(jnp.bfloat16)
    grad_gate, grad_up = lax.optimization_barrier((grad_gate, grad_up))
    total = contract_last(grad_gate, w_g) + contract_last(grad_up, w_u)
    next_input, previous_gradient = scatter(out, total.astype(jnp.bfloat16))
    return (next_input[None], previous_gradient[None])


def solution(mesh):
    rows = P("section", GROUP, None)
    weights = P("section", GROUP, None, None)
    return jax.shard_map(
        local,
        mesh=mesh,
        in_specs=(rows,) * 7 + (weights,) * 3,
        out_specs=(rows, rows),
        check_vma=False,
    )
```

```python
import functools
import math

import jax
import jax.numpy as jnp
from jax import lax
from jax.experimental import pallas as pl
from jax.experimental.pallas import tpu as pltpu
from jax.sharding import PartitionSpec as P

GROUP = ("node", "lane")
CORES = 2
MESH = pl.DeviceIdType.MESH


def position():
    node, lane = lax.axis_index("node"), lax.axis_index("lane")
    return node, lane // CORES, lane % CORES


def greet(peers):
    barrier = pltpu.get_barrier_semaphore()
    for cond, device in peers:
        @pl.when(cond)
        def _():
            pl.semaphore_signal(barrier, inc=1, device_id=device, device_id_type=MESH)
    pl.semaphore_wait(barrier, sum(jnp.where(cond, 1, 0) for cond, _ in peers))


def gather_kernel(n_node, n_x, count, *refs):
    ins, outs = refs[:count], refs[count : 2 * count]
    local_sem, recv, z_sem, x_sem, core_sem = refs[2 * count :]
    node, x, core = position()
    lane = x * CORES + core
    z_up, z_down = {"node": node + 1}, {"node": node - 1}
    x_up, x_down = {"lane": lane + CORES}, {"lane": lane - CORES}
    partner = {"lane": lane + 1 - 2 * core}
    has_up, has_down = node < n_node - 1, node > 0
    has_right, has_left = x < n_x - 1, x > 0
    greet(
        [
            (has_up, z_up),
            (has_down, z_down),
            (has_right, x_up),
            (has_left, x_down),
            (core < CORES, partner),
        ]
    )
    sends = []

    def send(cond, a, src, z, at_x, sem, device):
        where = outs[a].at[z, at_x * CORES + core]

        def copy():
            return pltpu.make_async_remote_copy(
                src_ref=where if src is None else src,
                dst_ref=where,
                send_sem=sem,
                recv_sem=recv.at[a, z, at_x * CORES + core],
                device_id=device,
                device_id_type=MESH,
            )

        @pl.when(cond)
        def _():
            copy().start()

        sends.append((cond, copy))

    def arrived(a, z, at_lane):
        where = outs[a].at[z, at_lane]
        pltpu.make_async_remote_copy(
            src_ref=where,
            dst_ref=where,
            send_sem=core_sem.at[a, 0, 0],
            recv_sem=recv.at[a, z, at_lane],
            device_id=partner,
            device_id_type=MESH,
        ).wait_recv()

    def along_x(cond, a, src, z):
        send(cond & has_right, a, src, z, x, x_sem.at[a, 0, z, x], x_up)
        send(cond & has_left, a, src, z, x, x_sem.at[a, 1, z, x], x_down)
        send(cond, a, src, z, x, core_sem.at[a, z, x], partner)

    always = core < CORES
    keeps = []
    for a in range(count):
        send(has_up, a, ins[a], node, x, z_sem.at[a, 0, node], z_up)
        send(has_down, a, ins[a], node, x, z_sem.at[a, 1, node], z_down)
        along_x(always, a, ins[a], node)
    for a in range(count):
        keep = pltpu.make_async_copy(ins[a], outs[a].at[node, lane], local_sem.at[a])
        keep.start()
        keeps.append(keep)
    for step in range(1, n_node):
        for a in range(count):
            below, above = node - step, node + step
            from_below, from_above = below >= 0, above < n_node

            @pl.when(from_below)
            def _():
                arrived(a, below, lane)

            send(from_below & has_up, a, None, below, x, z_sem.at[a, 0, below], z_up)
            along_x(from_below, a, None, below)

            @pl.when(from_above)
            def _():
                arrived(a, above, lane)

            send(from_above & has_down, a, None, above, x, z_sem.at[a, 1, above], z_down)
            along_x(from_above, a, None, above)
    for step in range(1, n_x):
        for a in range(count):
            for k in range(n_node):
                z = (node + k) % n_node
                for at_x, cond, go_on, way, device in (
                    (x - step, x - step >= 0, has_right, 0, x_up),
                    (x + step, x + step < n_x, has_left, 1, x_down),
                ):
                    @pl.when(cond)
                    def _():
                        arrived(a, z, at_x * CORES + core)

                    if n_x > 2:
                        send(cond & go_on, a, None, z, at_x, x_sem.at[a, way, z, at_x], device)
                    send(cond, a, None, z, at_x, core_sem.at[a, z, at_x], partner)
    for a in range(count):
        for k in range(n_node):
            for at_x in range(n_x):
                arrived(a, k, at_x * CORES + 1 - core)
    for cond, copy in sends:
        @pl.when(cond)
        def _():
            copy().wait_send()
    for keep in keeps:
        keep.wait()


def gather(*arrays):
    n_node, n_lane = lax.axis_size("node"), lax.axis_size("lane")
    n_x, count = n_lane // CORES, len(arrays)
    return pl.pallas_call(
        functools.partial(gather_kernel, n_node, n_x, count),
        out_shape=[jax.ShapeDtypeStruct((n_node, n_lane) + a.shape, a.dtype) for a in arrays],
        in_specs=[pl.BlockSpec(memory_space=pltpu.VMEM)] * count,
        out_specs=[pl.BlockSpec(memory_space=pl.ANY)] * count,
        scratch_shapes=[
            pltpu.SemaphoreType.DMA((count,)),
            pltpu.SemaphoreType.DMA((count, n_node, n_lane)),
            pltpu.SemaphoreType.DMA((count, 2, n_node)),
            pltpu.SemaphoreType.DMA((count, 2, n_node, n_x)),
            pltpu.SemaphoreType.DMA((count, n_node, n_x)),
        ],
        compiler_params=pltpu.CompilerParams(collective_id=0, has_side_effects=True),
    )(*arrays)


def scatter_kernel(n_section, n_node, n_x, count, *refs):
    parts, outs = refs[:count], refs[count : 2 * count]
    (own, core_in, x_in, z_in, final, local_sem, core_send, core_recv, x_send, x_recv, z_send,
     z_recv, y_send, y_recv) = refs[2 * count :]
    node, x, core = position()
    section = lax.axis_index("section")
    lane = x * CORES + core
    partner = {"lane": lane + 1 - 2 * core}
    z_up, z_down = {"node": node + 1}, {"node": node - 1}
    x_up, x_down = {"lane": lane + CORES}, {"lane": lane - CORES}
    after = {"section": (section + 1) % n_section}
    before = {"section": (section + n_section - 1) % n_section}
    has_up, has_down = node < n_node - 1, node > 0
    has_right, has_left = x < n_x - 1, x > 0
    always = core < CORES
    greet(
        [
            (has_up, z_up),
            (has_down, z_down),
            (has_right, x_up),
            (has_left, x_down),
            (always, partner),
            (always, after),
            (always, before),
        ]
    )

    def remote(src, dst, send_sem, recv_sem, device):
        return pltpu.make_async_remote_copy(
            src_ref=src,
            dst_ref=dst,
            send_sem=send_sem,
            recv_sem=recv_sem,
            device_id=device,
            device_id_type=MESH,
        )

    def add(target, *others):
        total = target[...].astype(jnp.float32)
        for other in others:
            total = total + other[...].astype(jnp.float32)
        target[...] = total.astype(target.dtype)

    sends = []

    def start(cond, make):
        @pl.when(cond)
        def _():
            make().start()

        sends.append((cond, make))

    owners = []
    for t in range(n_node - 1):
        owners.append((node + n_node - 1 - t, t >= node))
        owners.append((t + node - (n_node - 1), t + node >= n_node - 1))
    x_steps = [
        (t, x + n_x - 1 - t, t >= x, t + x - (n_x - 1), t + x >= n_x - 1) for t in range(n_x - 1)
    ]
    every = owners + [(node, always)]

    loads = []
    for a in range(count):
        load = pltpu.make_async_copy(parts[a].at[:, :, core], own.at[a], local_sem.at[a])
        load.start()
        loads.append(load)

    def core_copy(a, z, at_x):
        return remote(
            parts[a].at[z, at_x, 1 - core],
            core_in.at[a, z, at_x],
            core_send.at[a, z, at_x],
            core_recv.at[a, z, at_x],
            partner,
        )

    for a in range(count):
        for z, cond in every:
            for _, q_up, c_up, q_down, c_down in x_steps:
                start(cond & c_up, functools.partial(core_copy, a, z, q_up))
                start(cond & c_down, functools.partial(core_copy, a, z, q_down))
        for z, cond in every:
            start(cond, functools.partial(core_copy, a, z, x))

    def x_copy(a, z, q, slot, device):
        return remote(
            own.at[a, z, q], x_in.at[a, z, slot], x_send.at[a, z, q], x_recv.at[a, z, slot], device
        )

    def z_copy(a, z, slot, device):
        return remote(
            own.at[a, z, x], z_in.at[a, slot], z_send.at[a, z], z_recv.at[a, slot], device
        )

    for a in range(count):
        loads[a].wait()
        for z, cond in every:
            for t, q_up, c_up, q_down, c_down in x_steps:
                for q, c, more, slot, device in (
                    (q_up, c_up, has_left, q_up, x_up),
                    (q_down, c_down, has_right, None, x_down),
                ):
                    @pl.when(cond & c)
                    def _():
                        core_copy(a, z, q).wait_recv()
                        add(own.at[a, z, q], core_in.at[a, z, q])

                    if t > 0:
                        @pl.when(cond & c & more)
                        def _():
                            x_copy(a, z, q, q, partner).wait_recv()
                            add(own.at[a, z, q], x_in.at[a, z, q])

                    if slot is not None:
                        start(cond & c, functools.partial(x_copy, a, z, q, slot, device))
                    else:
                        near = q == x - 1
                        start(
                            cond & c & near, functools.partial(x_copy, a, z, q, n_x, device)
                        )
                        if n_x > 2:
                            start(
                                cond & c & (q < x - 1),
                                functools.partial(x_copy, a, z, q, q, device),
                            )

    def collect(a, z):
        core_copy(a, z, x).wait_recv()
        add(own.at[a, z, x], core_in.at[a, z, x])
        for c, slot in ((has_left, x), (has_right, n_x)):
            @pl.when(c)
            def _():
                x_copy(a, z, 0, slot, partner).wait_recv()
                add(own.at[a, z, x], x_in.at[a, z, slot])

    for a in range(count):
        for k, (z, cond) in enumerate(owners):
            going_up = k % 2 == 0

            @pl.when(cond)
            def _():
                collect(a, z)

            if k >= 2:
                @pl.when(cond & (has_down if going_up else has_up))
                def _():
                    z_copy(a, z, z, partner).wait_recv()
                    add(own.at[a, z, x], z_in.at[a, z])

            if going_up:
                start(cond, functools.partial(z_copy, a, z, z, z_up))
            else:
                start(cond & (z == node - 1), functools.partial(z_copy, a, z, n_node, z_down))
                if n_node > 2:
                    start(cond & (z < node - 1), functools.partial(z_copy, a, z, z, z_down))
        collect(a, node)

    def y_copy(a):
        return remote(
            final.at[a], outs[a], y_send.at[a], y_recv.at[a], after if a == 0 else before
        )

    for a in range(count):
        for c, slot in ((has_down, node), (has_up, n_node)):
            @pl.when(c)
            def _():
                z_copy(a, node, slot, partner).wait_recv()
                add(own.at[a, node, x], z_in.at[a, slot])
        final[a] = own[a, node, x]
        y_copy(a).start()
    for a in range(count):
        y_copy(a).wait()
    for cond, make in sends:
        @pl.when(cond)
        def _():
            make().wait_send()


def scatter(*parts):
    n_section, n_node = lax.axis_size("section"), lax.axis_size("node")
    n_x, count = lax.axis_size("lane") // CORES, len(parts)
    rows, width = parts[0].shape
    tok = rows // (n_node * n_x * CORES)
    dtype = parts[0].dtype
    block = (tok, width)
    dma = pltpu.SemaphoreType.DMA
    return pl.pallas_call(
        functools.partial(scatter_kernel, n_section, n_node, n_x, count),
        out_shape=[jax.ShapeDtypeStruct(block, dtype)] * count,
        in_specs=[pl.BlockSpec(memory_space=pl.ANY)] * count,
        out_specs=[pl.BlockSpec(memory_space=pltpu.VMEM)] * count,
        scratch_shapes=[
            pltpu.VMEM((count, n_node, n_x) + block, dtype),
            pltpu.VMEM((count, n_node, n_x) + block, dtype),
            pltpu.VMEM((count, n_node, n_x + 1) + block, dtype),
            pltpu.VMEM((count, n_node + 1) + block, dtype),
            pltpu.VMEM((count,) + block, dtype),
            dma((count,)),
            dma((count, n_node, n_x)),
            dma((count, n_node, n_x)),
            dma((count, n_node, n_x)),
            dma((count, n_node, n_x + 1)),
            dma((count, n_node)),
            dma((count, n_node + 1)),
            dma((count,)),
            dma((count,)),
        ],
        compiler_params=pltpu.CompilerParams(
            collective_id=1, has_side_effects=True, vmem_limit_bytes=67043328
        ),
    )(*(part.reshape((n_node, n_x, CORES) + block) for part in parts))


def coefficients(routes, gates, experts):
    hit = routes[:, :, None] == jnp.arange(experts, dtype=jnp.int32)[None, None, :]
    return jnp.sum(jnp.where(hit, gates[:, :, None], 0.0), axis=1)


def contract_last(a, b):
    return lax.dot_general(a, b, (((1,), (1,)), ((), ())), preferred_element_type=jnp.float32)


VMEM_BYTES = 64 * 2**20
ROW_TILE = 16
LANES = 128


def distance_order(n):
    return [sorted(range(n), key=lambda other: (abs(other - z), (z >= n // 2) != (other > z))) for z in range(n)]


def fused_kernel(shape, *refs):
    n_section, n_node, experts, tok, cross, split, plan = shape
    (f_in, f_routes, f_gates, b_in, cot_in, b_routes, b_gates, wg_in, wu_in, wd_in) = refs[:10]
    outs = refs[10:12]
    (rows, coefs, routes, gates, w_g, w_u, w_d, w_gt, w_ut, w_dt, hid_a, hid_b) = refs[12:24]
    n_items = 3
    parts, core_in, x_in, z_in, last = (refs[24 + n_items * k : 24 + n_items * (k + 1)] for k in range(5))
    (ls, zs, zr, xs, xr, cs, cr, es, er, rs, rr, hs, hr, ys, yr) = refs[24 + 5 * n_items :]
    half = tok // 2
    node, x, core = position()
    section = lax.axis_index("section")
    lane = x * CORES + core
    me = node * (2 * CORES) + lane
    z_up, z_down = {"node": node + 1}, {"node": node - 1}
    beside = {"lane": (1 - x) * CORES + core}
    partner = {"lane": lane + 1 - 2 * core}
    after = {"section": (section + 1) % n_section}
    before = {"section": (section + n_section - 1) % n_section}
    has_up, has_down = node < n_node - 1, node > 0
    always = core < CORES
    order = distance_order(n_node)

    def near(k):
        found = order[0][k]
        for z in range(1, n_node):
            found = jnp.where(node == z, order[z][k], found)
        return found

    loads = []

    def load(src, dst):
        loads.append(pltpu.make_async_copy(src, dst, ls.at[len(loads)]))
        loads[-1].start()
        return loads[-1]

    small = [
        load(f_routes, routes.at[0]),
        load(b_routes, routes.at[1]),
        load(f_gates, gates.at[0]),
        load(b_gates, gates.at[1]),
    ]
    own = [[load(f_in, rows.at[0, node, x, core])]]
    for h in range(2):
        own.append(
            [
                load(b_in.at[pl.ds(h * half, half)], rows.at[1 + h, node, x, core, pl.ds(0, half)]),
                load(cot_in.at[pl.ds(h * half, half)], rows.at[1 + h, node, x, core, pl.ds(half, half)]),
            ]
        )
    weights = [load(wg_in, w_g), load(wu_in, w_u), load(wd_in, w_d)]

    for copy in small:
        copy.wait()
    groups = LANES // (2 * experts)
    held = tok // groups
    top = routes.shape[1]
    lists = [routes[0].astype(jnp.float32), routes[1].astype(jnp.float32), gates[0], gates[1]]
    lists = jnp.concatenate(lists, axis=0)
    lists = jnp.concatenate([lists, jnp.zeros((4 * top, LANES - tok), jnp.float32)], axis=1)
    lists = jnp.concatenate([lists, jnp.zeros((LANES - 4 * top, LANES), jnp.float32)], axis=0).T
    at = lax.broadcasted_iota(jnp.int32, (held, LANES), 1).astype(jnp.float32)
    packed = jnp.zeros((held, LANES), jnp.float32)
    for which in range(2):
        for g in range(groups):
            some = lists[g * held : (g + 1) * held]
            for k in range(top):
                slot = which * top + k
                chosen = at == some[:, slot : slot + 1] + float((g * 2 + which) * experts)
                packed = packed + jnp.where(chosen, some[:, 2 * top + slot : 2 * top + slot + 1], 0.0)
    coefs[node, x, core] = packed

    greet(
        [
            (has_up, z_up),
            (has_down, z_down),
            (always, beside),
            (always, partner),
            (always, after),
            (always, before),
        ]
    )

    pending = []

    def remote(src, dst, send_sem, recv_sem, device):
        return pltpu.make_async_remote_copy(
            src_ref=src, dst_ref=dst, send_sem=send_sem, recv_sem=recv_sem,
            device_id=device, device_id_type=MESH,
        )

    def start(cond, make):
        if cond is None:
            make().start()
        else:
            @pl.when(cond)
            def _():
                make().start()
        pending.append((cond, make))

    def drain(keep=0):
        while len(pending) > keep:
            cond, make = pending.pop(0)
            if cond is None:
                make().wait_send()
            else:
                @pl.when(cond)
                def _():
                    make().wait_send()

    n_coef = n_items
    T1 = pl.ds(0, tok - cross)
    T2 = pl.ds(tok - cross, cross)

    def block(i, z, at_x, at_core=None):
        at_core = core if at_core is None else at_core
        return coefs.at[z, at_x, at_core] if i == n_coef else rows.at[i, z, at_x, at_core]

    def z_piece(i, z, p):
        return rows.at[i, z, 1 - x, core, T2] if p else block(i, z, x)

    def x_piece(i, z, at_x, whole):
        return block(i, z, at_x) if whole or i == n_coef else rows.at[i, z, at_x, core, T1]

    def z_copy(i, z, p, slot, device):
        where = z_piece(i, z, p)
        return remote(where, where, zs.at[i, slot, p], zr.at[i, z, p], device)

    def x_copy(i, z, at_x, whole):
        where = x_piece(i, z, at_x, whole)
        return remote(where, where, xs.at[i, z], xr.at[i, z], beside)

    def c_copy(i, z, at_x, at_core, q):
        where = block(i, z, at_x, at_core)
        return remote(where, where, cs.at[i, z, q], cr.at[i, z, q], partner)

    both = functools.partial

    def along_z(i, z, p):
        start(has_up, both(z_copy, i, z, p, z, z_up))
        start(has_down, both(z_copy, i, z, p, n_node, z_down))

    def members(i):
        return (n_coef, i) if i == 0 else (i,)

    def sides(j):
        return (
            (node - j, node - j >= 0, has_up, z_up),
            (node + j, node + j < n_node, has_down, z_down),
        )

    def arrive_z(i, j):
        if j == 0:
            for copy in own[i]:
                copy.wait()
            for m in members(i):
                along_z(m, node, 0)
                start(None, both(x_copy, m, node, x, True))
                start(None, both(c_copy, m, node, x, core, 0))
            return
        for z, there, go, device in sides(j):
            for m in members(i):
                @pl.when(there)
                def _():
                    z_copy(m, z, 0, z, device).wait_recv()

                start(there & go, both(z_copy, m, z, 0, z, device))
                start(there, both(x_copy, m, z, x, False))
                start(there, both(c_copy, m, z, x, core, 0))

    def relay_other(i, j):
        for z, there, go, device in sides(j):
            @pl.when(there)
            def _():
                z_copy(i, z, 1, z, device).wait_recv()

            start(there & go, both(z_copy, i, z, 1, z, device))

    def arrive_x(i, j):
        if j == 0:
            for m in members(i):
                x_copy(m, node, 1 - x, True).wait_recv()
                if m != n_coef:
                    along_z(m, node, 1)
                start(None, both(c_copy, m, node, 1 - x, core, 1))
            return
        for z, there, _, _ in sides(j):
            for m in members(i):
                @pl.when(there)
                def _():
                    x_copy(m, z, 1 - x, False).wait_recv()

                start(there, both(c_copy, m, z, 1 - x, core, 1))

    def exchange(i, z, at_x):
        return remote(
            parts[i].at[z, at_x, 1 - core], core_in[i].at[z, at_x],
            es.at[i, z, at_x], er.at[i, z, at_x], partner,
        )

    def coef_of(z, which, first, count):
        where = lax.broadcasted_iota(jnp.int32, (held, LANES), 1)
        columns = []
        for at_x in range(2):
            for at_core in range(CORES):
                values = coefs[z, at_x, at_core]
                for g in range(first // held, (first + count) // held):
                    wanted = where == g * (2 * experts) + which * experts + me
                    columns.append(jnp.sum(jnp.where(wanted, values, 0.0), axis=1, keepdims=True))
        return jnp.concatenate(columns, axis=0)

    ff, width = w_d.shape
    wide = width // 2

    def turn():
        for copy in weights:
            copy.wait()

        @pl.loop(0, width // 256)
        def _(j):
            js = pl.ds(pl.multiple_of(j * 256, 256), 256)
            w_gt[:, js] = w_g[js, :].T
            w_ut[:, js] = w_u[js, :].T
            w_dt[js, :] = w_d[:, js].T

    def forward(z):
        count = 2 * CORES * tok
        coef = coef_of(z, 0, 0, tok)
        v = rows[0, z].reshape(count, width)
        a = jnp.dot(v, w_g[...], preferred_element_type=jnp.float32)
        b = jnp.dot(v, w_u[...], preferred_element_type=jnp.float32)
        hid_a[...] = (a / (1.0 + jnp.exp(-a)) * b).astype(jnp.bfloat16)

        @pl.loop(0, width // wide)
        def _(j):
            js = pl.ds(pl.multiple_of(j * wide, wide), wide)
            out = jnp.dot(hid_a[...], w_d[:, js], preferred_element_type=jnp.float32) * coef
            parts[0][z, :, :, :, js] = out.astype(jnp.bfloat16).reshape(2, CORES, tok, wide)

    def backward(i, z):
        count = 2 * CORES * half
        coef = coef_of(z, 1, (i - 1) * half, half)
        v = rows[i, z, :, :, 0:half].reshape(count, width)
        g = rows[i, z, :, :, half:].reshape(count, width)
        a = jnp.dot(v, w_g[...], preferred_element_type=jnp.float32)
        b = jnp.dot(v, w_u[...], preferred_element_type=jnp.float32)
        h = jnp.dot(g, w_dt[...], preferred_element_type=jnp.float32) * coef
        q = 1.0 / (1.0 + jnp.exp(-a))
        hid_a[0:count] = (h * b * q * (1.0 + a * (1.0 - q))).astype(jnp.bfloat16)
        hid_b[0:count] = (h * a * q).astype(jnp.bfloat16)

        @pl.loop(0, width // wide)
        def _(j):
            js = pl.ds(pl.multiple_of(j * wide, wide), wide)
            total = jnp.dot(hid_a[0:count], w_gt[:, js], preferred_element_type=jnp.float32)
            total = total + jnp.dot(hid_b[0:count], w_ut[:, js], preferred_element_type=jnp.float32)
            parts[i][z, :, :, :, js] = total.astype(jnp.bfloat16).reshape(2, CORES, half, wide)

    def compute(i, k):
        z = near(k)
        for m in members(i):
            c_copy(m, z, x, 1 - core, 0).wait_recv()
            c_copy(m, z, 1 - x, 1 - core, 1).wait_recv()
        forward(z) if i == 0 else backward(i, z)
        for at_x in (1 - x, x):
            start(None, both(exchange, i, z, at_x))

    def total_of(*terms):
        total = terms[0].astype(jnp.float32)
        for term in terms[1:]:
            total = total + term.astype(jnp.float32)
        return total.astype(jnp.bfloat16)

    def some(i, p):
        size = (tok if i == 0 else half) // split[i]
        return pl.ds(p * size, size)

    def r_copy(i, z, p):
        return remote(
            parts[i].at[z, 1 - x, core, some(i, p)], x_in[i].at[z, some(i, p)],
            rs.at[i, z, p], rr.at[i, z, p], beside,
        )

    def cross_x(i, k):
        z = near(k)
        exchange(i, z, 1 - x).wait_recv()
        for p in range(split[i]):
            r = some(i, p)
            parts[i][z, 1 - x, core, r] = total_of(parts[i][z, 1 - x, core, r], core_in[i][z, 1 - x, r])
            start(None, both(r_copy, i, z, p))

    def h_copy(i, z, way, p):
        return remote(
            parts[i].at[z, x, core, some(i, p)], z_in[i].at[way, z, some(i, p)],
            hs.at[i, z, p], hr.at[i, way, z, p], (z_up, z_down)[way],
        )

    def y_copy(i, p):
        size = (tok if i == 0 else half) // split[i]
        where = pl.ds((0 if i == 0 else (i - 1) * half) + p * size, size)
        return remote(
            last[i].at[some(i, p)], outs[min(i, 1)].at[where], ys.at[i, p], yr.at[i, p],
            after if i == 0 else before,
        )

    def chain(i, s, p=0):
        r = some(i, p)

        def mine(z):
            return [parts[i][z, x, core, r], core_in[i][z, x, r], x_in[i][z, r]]

        if s == n_node - 1:
            if p == 0:
                exchange(i, node, x).wait_recv()
            r_copy(i, node, p).wait_recv()
            for ways, there in (((0,), node == n_node - 1), ((1,), node == 0), ((0, 1), has_down & has_up)):
                @pl.when(there)
                def _():
                    for way in ways:
                        h_copy(i, node, way, p).wait_recv()
                    last[i][r] = total_of(*mine(node), *[z_in[i][way, node, r] for way in ways])

            y_copy(i, p).start()
            return
        for way, z, there, more in (
            (0, n_node - 1 + node - s, s >= node, has_down),
            (1, s + node - (n_node - 1), s + node >= n_node - 1, has_up),
        ):
            @pl.when(there)
            def _():
                if p == 0:
                    exchange(i, z, x).wait_recv()
                r_copy(i, z, p).wait_recv()

            @pl.when(there & more)
            def _():
                h_copy(i, z, way, p).wait_recv()
                parts[i][z, x, core, r] = total_of(*mine(z), z_in[i][way, z, r])

            @pl.when(there & (node == (n_node - 1) * way))
            def _():
                parts[i][z, x, core, r] = total_of(*mine(z))

            start(there, both(h_copy, i, z, way, p))

    for step in plan:
        kind, i, k = step
        if kind == "D":
            drain(k)
        elif kind == "W":
            turn()
        elif kind == "I":
            chain(i, k, 1)
        else:
            {"A": arrive_z, "T": relay_other, "X": arrive_x, "C": compute, "R": cross_x, "H": chain}[kind](i, k)
    drain()
    for i in range(n_items):
        for p in range(split[i]):
            y_copy(i, p).wait()


SPLIT = (1, 1, 2)
ORDER = (
    "A00 A10 W00 X00",
    "A01 C00 R00 T01",
    "X01 A11 C01 A02",
    "R01 T02 X10 A20",
    "X02 C02 C10 A03",
    "R02 R10 T03 X03",
    "T11 A12 X11 C03",
    "X20 A21 C20 R03",
    "C11 T12 A13 X12",
    "C12 T21 R11 H00",
    "X21 R12 C21 A22",
    "H01 T13 R20 X13",
    "C13 T22 H02 R13",
    "X22 A23 C22 T23",
    "H10 R21 H11 X23",
    "R22 C23 H12 R23",
    "H03 H20 I20 H21",
    "H13 I21 H22 I22",
    "H23 I23",
)


def schedule():
    steps = [step for line in ORDER for step in line.split()]
    return tuple((step[0], int(step[1]), int(step[2:])) for step in steps)


def fused_scratch(n_node, experts, tok, width, ff, top):
    half = tok // 2
    heights = (tok, half, half)
    bf16 = jnp.bfloat16
    held = tok * 2 * experts // LANES
    most = 2 * CORES * tok
    items = len(heights)

    def each(*lead):
        return [(lead + (height, width), bf16) for height in heights]

    buffers = [
        ((items, n_node, 2, CORES, tok, width), bf16),
        ((n_node, 2, CORES, held, LANES), jnp.float32),
        ((2, top, tok), jnp.int32),
        ((2, top, tok), jnp.float32),
        ((width, ff), bf16),
        ((width, ff), bf16),
        ((ff, width), bf16),
        ((ff, width), bf16),
        ((ff, width), bf16),
        ((width, ff), bf16),
        ((most, ff), bf16),
        ((most, ff), bf16),
    ]
    buffers += each(n_node, 2, CORES) + each(n_node, 2) + each(n_node) + each(2, n_node) + each()
    semaphores = [
        (12,),
        (items + 1, n_node + 1, 2),
        (items + 1, n_node, 2),
        (items + 1, n_node),
        (items + 1, n_node),
        (items + 1, n_node, 2),
        (items + 1, n_node, 2),
        (items, n_node, 2),
        (items, n_node, 2),
        (items, n_node, 2),
        (items, n_node, 2),
        (items, n_node, 2),
        (items, 2, n_node, 2),
        (items, 2),
        (items, 2),
    ]
    return buffers, semaphores


def fits(n_node, n_x, experts, tok, width, ff, top):
    if n_x != 2 or n_node != 4 or tok % (4 * ROW_TILE) or ff % 256 or width % 512:
        return False
    if LANES % (2 * experts) or tok % (LANES // (2 * experts)):
        return False
    held = tok * 2 * experts // LANES
    if held % 8 or (tok // 2) % held or tok > LANES or 4 * top > LANES:
        return False
    buffers, _ = fused_scratch(n_node, experts, tok, width, ff, top)
    return sum(math.prod(shape) * jnp.dtype(kind).itemsize for shape, kind in buffers) < VMEM_BYTES * 7 // 8


def settle_kernel(count, *refs):
    srcs, dsts, sem = refs[:count], refs[count : 2 * count], refs[2 * count]
    copies = [pltpu.make_async_copy(srcs[k], dsts[k], sem.at[k]) for k in range(count)]
    for copy in copies:
        copy.start()
    for copy in copies:
        copy.wait()


def settle(*arrays):
    count = len(arrays)
    return pl.pallas_call(
        functools.partial(settle_kernel, count),
        out_shape=[jax.ShapeDtypeStruct(a.shape, a.dtype) for a in arrays],
        in_specs=[pl.BlockSpec(memory_space=pltpu.VMEM)] * count,
        out_specs=[pl.BlockSpec(memory_space=pl.ANY)] * count,
        scratch_shapes=[pltpu.SemaphoreType.DMA((count,))],
    )(*arrays)


def fused(arrays, n_section, n_node, experts):
    tok, width = arrays[0].shape
    top, ff = arrays[1].shape[0], arrays[7].shape[1]
    buffers, semaphores = fused_scratch(n_node, experts, tok, width, ff, top)
    shape = (n_section, n_node, experts, tok, tok // 2, SPLIT, schedule())
    return pl.pallas_call(
        functools.partial(fused_kernel, shape),
        out_shape=[jax.ShapeDtypeStruct((tok, width), jnp.bfloat16)] * 2,
        in_specs=[pl.BlockSpec(memory_space=pl.ANY)] * len(arrays),
        out_specs=[pl.BlockSpec(memory_space=pltpu.VMEM)] * 2,
        scratch_shapes=[pltpu.VMEM(*buffer) for buffer in buffers]
        + [pltpu.SemaphoreType.DMA(count) for count in semaphores],
        compiler_params=pltpu.CompilerParams(
            collective_id=2, has_side_effects=True, vmem_limit_bytes=67043328
        ),
    )(*arrays)


def local(
    forward_input,
    forward_routes,
    forward_gates,
    backward_input,
    backward_cotangent,
    backward_routes,
    backward_gates,
    w_gate,
    w_up,
    w_down,
):
    experts = lax.axis_size("node") * lax.axis_size("lane") * w_gate.shape[1]
    w_g, w_u, w_d = w_gate[0, 0], w_up[0, 0], w_down[0, 0]
    n_node, n_x = lax.axis_size("node"), lax.axis_size("lane") // CORES
    tok, width, top, ff = *forward_input.shape[1:], forward_routes.shape[2], w_g.shape[1]
    if w_gate.shape[1] == 1 and fits(n_node, n_x, experts, tok, width, ff, top):
        mine = (forward_input[0], forward_routes[0].T, forward_gates[0].T, backward_input[0],
                backward_cotangent[0], backward_routes[0].T, backward_gates[0].T, w_g, w_u, w_d)
        outs = settle(*fused(mine, lax.axis_size("section"), n_node, experts))
        return (outs[0][None], outs[1][None])
    me = lax.axis_index(GROUP)

    coef = jnp.concatenate(
        [
            coefficients(forward_routes[0], forward_gates[0], experts),
            coefficients(backward_routes[0], backward_gates[0], experts),
        ],
        axis=1,
    )
    coef = jnp.pad(coef, ((0, 0), (0, -coef.shape[1] % 128)))
    tokens = forward_input.shape[1] * lax.axis_size("node") * lax.axis_size("lane")
    coef, fwd, bwd, cot = (
        array.reshape(tokens, -1)
        for array in gather(coef, forward_input[0], backward_input[0], backward_cotangent[0])
    )
    fwd_coef = lax.dynamic_slice_in_dim(coef, me, 1, axis=1)
    bwd_coef = lax.dynamic_slice_in_dim(coef, experts + me, 1, axis=1)

    pre_gate = jnp.dot(fwd, w_g, preferred_element_type=jnp.float32)
    pre_up = jnp.dot(fwd, w_u, preferred_element_type=jnp.float32)
    hidden = (jax.nn.silu(pre_gate) * pre_up).astype(jnp.bfloat16)
    hidden = lax.optimization_barrier(hidden)
    out = jnp.dot(hidden, w_d, preferred_element_type=jnp.float32)
    out = (out * fwd_coef).astype(jnp.bfloat16)

    pre_gate = jnp.dot(bwd, w_g, preferred_element_type=jnp.float32)
    pre_up = jnp.dot(bwd, w_u, preferred_element_type=jnp.float32)
    grad_hidden = contract_last(cot, w_d) * bwd_coef
    sigma = jax.nn.sigmoid(pre_gate)
    grad_gate = (grad_hidden * pre_up * sigma * (1.0 + pre_gate * (1.0 - sigma))).astype(
        jnp.bfloat16
    )
    grad_up = (grad_hidden * pre_gate * sigma).astype(jnp.bfloat16)
    grad_gate, grad_up = lax.optimization_barrier((grad_gate, grad_up))
    total = contract_last(grad_gate, w_g) + contract_last(grad_up, w_u)
    next_input, previous_gradient = scatter(out, total.astype(jnp.bfloat16))
    return (next_input[None], previous_gradient[None])


def solution(mesh):
    rows = P("section", GROUP, None)
    weights = P("section", GROUP, None, None)
    return jax.shard_map(
        local,
        mesh=mesh,
        in_specs=(rows,) * 7 + (weights,) * 3,
        out_specs=(rows, rows),
        check_vma=False,
    )
```
